256 devices in a mesh: kv: 8 (over y, x_hi), sp: 32 (over z, x_lo, core).
Axes of the slice: x: 4 (x_hi: 2, x_lo: 2; x = x_hi * 2 + x_lo), y: 4, z: 8, core: 2. Of those that a mesh axis runs over, the one named last changes fastest.
Arguments:
- queries: bfloat16 [4096, 4096], P('sp'), may hold values from -1.1953125 to 1.1953125
- keys: bfloat16 [16384, 4096], P(('kv', 'sp')), may hold values from -1.1953125 to 1.1953125
- values: bfloat16 [16384, 4096], P(('kv', 'sp')), may hold values from -6 to 6
- outputs: bfloat16 [4096, 4096], P('sp'), may hold values from -6 to 6
- out_grad: bfloat16 [4096, 4096], P('sp'), may hold values from -1536 to 1536
- stats: float32 [4096, 32], P('sp'), may hold values from -1 to 1
Outputs:
- query_grad: float32 [4096, 4096], P(('kv', 'sp'))
- key_grad: float32 [16384, 4096], P(('kv', 'sp'))
- value_grad: float32 [16384, 4096], P(('kv', 'sp'))
The draws below stay inside these ranges and needn't reach their ends.
All inputs are finite; a program needn't handle non-finite values.
Results may differ from the reference program's by a relative error of at most 0.0029.
Values may be sent and summed in bfloat16 or wider, within the bound.
No kernel may reach another device: no remote copies, remote signals or barrier semaphores. Data moves between devices by JAX's collectives and lax.ppermute only.
A program may use at most 64 MiB of HBM per device.

```python
import math
import jax
import jax.numpy as jnp
from jax import lax

H = 32
DH = 128
QLEN = 4096
KEYS = 16384
N_KV = 8


def levels(rng, dims, cuts, smallest, largest):
    level, own = 1.0, jax.random.fold_in(rng, 6)
    for position, parts in cuts:
        draws = jnp.exp(jax.random.uniform(jax.random.fold_in(own, position), (parts,), jnp.float32, smallest / len(cuts), largest / len(cuts)))
        level = level * jnp.repeat(draws, dims[position] // parts).reshape([-1 if axis == position else 1 for axis in range(len(dims))])
    return level


def bell_draw(stream_key, shape, width, most, shards=(), held_as=jnp.bfloat16):
    factor_of = levels(stream_key, shape, shards, -0.22, 0.18) if shards else 1.0
    values = jax.random.normal(stream_key, shape, jnp.float32) * width * factor_of
    return jnp.minimum(jnp.maximum(values, -most), most).astype(held_as)


def setup_inputs(seed: int = 0) -> dict:
    key_list = jax.random.split(jax.random.key(seed), 7)
    queries = jnp.clip(jax.random.uniform(key_list[0], (QLEN, H * DH), jnp.float32, -1.1953125, 1.1953125) * levels(key_list[0], (QLEN, H * DH), ((0, 32),), -0.4, 0.0), -1.1953125, 1.1953125).astype(jnp.bfloat16)
    keys = jnp.clip(jax.random.uniform(key_list[1], (KEYS, H * DH), jnp.float32, -1.1953125, 1.1953125) * levels(key_list[1], (KEYS, H * DH), ((0, 256),), -0.4, 0.0), -1.1953125, 1.1953125).astype(jnp.bfloat16)
    values = bell_draw(key_list[2], (KEYS, H * DH), 1.0, 6.0, ((0, 256),))
    outputs = bell_draw(key_list[3], (QLEN, H * DH), 1.0, 6.0, ((0, 32),))
    out_grad = bell_draw(key_list[4], (QLEN, H * DH), (32 * N_KV), 1536.0, ((0, 32),))
    stats = jnp.clip(jax.random.uniform(key_list[5], (QLEN, H), jnp.float32, -1.0, 1.0) * levels(key_list[5], (QLEN, H), ((0, 32),), -0.4, 0.0), -1.0, 1.0)
    return {"queries": queries, "keys": keys, "values": values, "outputs": outputs, "out_grad": out_grad, "stats": stats}


def head_major(array):
    return jnp.transpose(array.reshape(array.shape[0], H, DH), (1, 0, 2))

def reference(queries, keys, values, outputs, out_grad, stats):
    inverse_root = 1.0 / math.sqrt(DH)
    delta = lax.optimization_barrier(jnp.sum(out_grad.astype(jnp.float32).reshape(QLEN, H, DH) * outputs.astype(jnp.float32).reshape(QLEN, H, DH), axis=2))

    def one_head(pieces):
        query_head, key_head, value_head, grad_head, stats_head, delta_head = pieces
        query_wide = query_head.astype(jnp.float32)
        key_wide = key_head.astype(jnp.float32)
        value_wide = value_head.astype(jnp.float32)
        grad_wide = grad_head.astype(jnp.float32)
        scores = jnp.dot(query_wide, key_wide.T, preferred_element_type=jnp.float32) * inverse_root
        probs = jnp.exp(scores - stats_head[:, None]) / KEYS
        probs_low = probs.astype(jnp.bfloat16).astype(jnp.float32)
        value_out = jnp.dot(probs_low.T, grad_wide, preferred_element_type=jnp.float32)
        prob_grad = jnp.dot(grad_wide, value_wide.T, preferred_element_type=jnp.float32)
        score_grad = (probs * (prob_grad - delta_head[:, None])).astype(jnp.bfloat16).astype(jnp.float32)
        query_out = jnp.dot(score_grad, key_wide, preferred_element_type=jnp.float32) * inverse_root
        key_out = jnp.dot(score_grad.T, query_wide, preferred_element_type=jnp.float32) * inverse_root
        return (query_out, key_out, value_out)
    query_all, key_all, value_all = lax.map(one_head, (head_major(queries), head_major(keys), head_major(values), head_major(out_grad), jnp.transpose(stats), jnp.transpose(delta)))
    query_grad = jnp.transpose(query_all, (1, 0, 2)).reshape(QLEN, H * DH)
    key_grad = jnp.transpose(key_all, (1, 0, 2)).reshape(KEYS, H * DH)
    value_grad = jnp.transpose(value_all, (1, 0, 2)).reshape(KEYS, H * DH)
    return (query_grad, key_grad, value_grad)
```

```python
import functools
import math

import jax
import jax.numpy as jnp
from jax import lax
from jax.experimental import pallas as pl
from jax.experimental.pallas import tpu as pltpu
from jax.sharding import Mesh
from jax.sharding import PartitionSpec as P

H = 32
DH = 128
QLEN = 4096
KLEN = 2048
NY, NX, NZ = 4, 2, 8
SP = ("z", "xl", "c")
ALL = ("y", "xh", "z", "xl", "c")
NSP = 32
ROWS = QLEN // NSP
SHARE = ROWS // NY
WIDE = 2 * SHARE + 8
KROWS = KLEN // NSP
QB = QLEN // (NY * NX)
OUT_ROWS = 2 * KROWS + QB // NSP
LOG2E = math.log2(math.e)
ROOT = 1.0 / math.sqrt(DH)
F32 = jnp.float32
BF16 = jnp.bfloat16


def dot(a, b, dims):
    return lax.dot_general(a, b, ((dims[0], dims[1]), ((), ())), preferred_element_type=F32)


def three(x):
    hi = x.astype(BF16).astype(F32)
    mid = (x - hi).astype(BF16).astype(F32)
    return hi, mid, x - hi - mid


def pack_queries(at_ref, q_ref, g_ref, o_ref, s_ref, out_ref):
    cols = []
    for h in range(H):
        c = slice(h * DH, (h + 1) * DH)
        out_ref[h, 0:SHARE, :] = q_ref[:, c]
        out_ref[h, SHARE : 2 * SHARE, :] = g_ref[:, c]
        prod = g_ref[:, c].astype(F32) * o_ref[:, c].astype(F32)
        cols.append(jnp.sum(prod, axis=1, keepdims=True))
    delta = jnp.transpose(jnp.concatenate(cols, axis=1))
    stats = jnp.transpose(s_ref[...])
    zero = jnp.zeros((H, DH - 3 * SHARE), F32)
    st = jnp.concatenate([*three(stats), zero], axis=1)
    de = jnp.concatenate([*three(delta), zero], axis=1)
    row = lax.broadcasted_iota(jnp.int32, (H, 8, DH), 1)
    out_ref[:, 2 * SHARE : WIDE, :] = jnp.where(
        row == 0, st[:, None, :], de[:, None, :]
    ).astype(BF16)


def packed_queries(at, queries, out_grad, outputs, stats):
    wide = pl.BlockSpec((SHARE, H * DH), lambda i, at: (at[0], 0))
    return pl.pallas_call(
        pack_queries,
        grid_spec=pltpu.PrefetchScalarGridSpec(
            num_scalar_prefetch=1,
            grid=(1,),
            in_specs=[wide, wide, wide, pl.BlockSpec((SHARE, H), lambda i, at: (at[0], 0))],
            out_specs=pl.BlockSpec((H, WIDE, DH), lambda i, at: (0, 0, 0)),
        ),
        out_shape=jax.ShapeDtypeStruct((H, WIDE, DH), BF16),
        cost_estimate=pl.CostEstimate(flops=10**6, bytes_accessed=2 * 10**6, transcendentals=0),
        name="pack_queries",
    )(at, queries, out_grad, outputs, stats)


def pack_keys(k_ref, v_ref, out_ref):
    for h in range(H):
        c = slice(h * DH, (h + 1) * DH)
        out_ref[h, 0:KROWS, :] = k_ref[:, c]
        out_ref[h, KROWS : 2 * KROWS, :] = v_ref[:, c]


def packed_keys(keys, values):
    return pl.pallas_call(
        pack_keys,
        out_shape=jax.ShapeDtypeStruct((H, 2 * KROWS, DH), BF16),
        cost_estimate=pl.CostEstimate(flops=10**6, bytes_accessed=2 * 10**6, transcendentals=0),
        name="pack_keys",
    )(keys, values)


def grads(steps, first, last, tab, *refs):
    parts = refs[:NY]
    st_ref, de_ref, kv_ref = refs[NY : NY + 3]
    rest = refs[NY + 3 :]
    if first:
        dq_ref, dk_ref, dv_ref = rest[:3]
        rest = rest[3:]

        @pl.when(pl.program_id(0) == 0)
        def _():
            dk_ref[...] = jnp.zeros_like(dk_ref)
            dv_ref[...] = jnp.zeros_like(dv_ref)

    else:
        dk_in, dv_in, dq_ref, dk_ref, dv_ref = rest[:5]
        rest = rest[5:]

        @pl.when(pl.program_id(0) == 0)
        def _():
            dk_ref[...] = dk_in[...]
            dv_ref[...] = dv_in[...]

    q = jnp.concatenate([p[0, :, 0:SHARE, :].reshape(-1, DH) for p in parts], axis=0)
    g = jnp.concatenate([p[0, :, SHARE : 2 * SHARE, :].reshape(-1, DH) for p in parts], axis=0)
    st = st_ref[0]
    de = de_ref[0]
    per = 8
    bk = per * KROWS
    total = None
    for j in range(KLEN // bk):
        k = kv_ref[j * per : (j + 1) * per, 0:KROWS, :].reshape(bk, DH)
        v = kv_ref[j * per : (j + 1) * per, KROWS : 2 * KROWS, :].reshape(bk, DH)
        rows = slice(j * bk, (j + 1) * bk)
        p = jnp.exp2(dot(k, q, ((1,), (1,))) * (ROOT * LOG2E) - st)
        ds = (p * (dot(v, g, ((1,), (1,))) - de)).astype(BF16)
        dv_ref[rows, :] += dot(p.astype(BF16), g, ((1,), (0,)))
        dk_ref[rows, :] += dot(ds, q, ((1,), (0,)))
        part = dot(ds, k, ((0,), (0,)))
        total = part if total is None else total + part
    total = total.reshape(NY, 4, SHARE, DH)
    for b in range(NY):
        dq_ref[0, :, b, :, :] = total[b].astype(dq_ref.dtype)
    if last:
        out_ref = rest[0]
        out_ref[:, 0:KROWS, :] = (dk_ref[...] * (ROOT / (KLEN * NY * NX))).astype(BF16).reshape(
            NSP, KROWS, DH
        )
        out_ref[:, KROWS : 2 * KROWS, :] = (dv_ref[...] * (1.0 / (KLEN * NY * NX))).astype(
            BF16
        ).reshape(NSP, KROWS, DH)


def grads_call(steps, first, last, dq_type, tab, big, st, de, kv, sums):
    def part(b):
        return pl.BlockSpec((1, 4, WIDE, DH), lambda i, t: (t[2 + b], t[i], 0, 0))

    vec = pl.BlockSpec((1, 1, QB), lambda i, t: (t[i], 0, 0))
    whole = pl.BlockSpec((KLEN, DH), lambda i, t: (0, 0))
    in_specs = [part(b) for b in range(NY)] + [
        vec,
        vec,
        pl.BlockSpec((NSP, 2 * KROWS, DH), lambda i, t: (0, 0, 0)),
    ]
    dq_spec = pl.BlockSpec((1, 4, NY, SHARE, DH), lambda i, t: (i, 0, 0, 0, 0))
    out_shape = [
        jax.ShapeDtypeStruct((steps, 4, NY, SHARE, DH), dq_type),
        jax.ShapeDtypeStruct((KLEN, DH), F32),
        jax.ShapeDtypeStruct((KLEN, DH), F32),
    ]
    out_specs = [dq_spec, whole, whole]
    aliases = {}
    if not first:
        in_specs += [whole, whole]
        aliases = {NY + 4: 1, NY + 5: 2}
    if last:
        out_shape.append(jax.ShapeDtypeStruct((NSP, OUT_ROWS, DH), BF16))
        out_specs.append(pl.BlockSpec((NSP, OUT_ROWS, DH), lambda i, t: (0, 0, 0)))
    pairs = steps * QB * KLEN
    return pl.pallas_call(
        functools.partial(grads, steps, first, last),
        grid_spec=pltpu.PrefetchScalarGridSpec(
            num_scalar_prefetch=1, grid=(steps,), in_specs=in_specs, out_specs=out_specs
        ),
        out_shape=out_shape,
        input_output_aliases=aliases,
        compiler_params=pltpu.CompilerParams(vmem_limit_bytes=48 << 20),
        cost_estimate=pl.CostEstimate(
            flops=pairs * 10 * DH, bytes_accessed=6 << 20, transcendentals=pairs
        ),
        name="grads",
    )(tab, *([big] * NY), st, de, kv, *sums)


def shift(x, axis, by):
    n = lax.axis_size(axis)
    return lax.ppermute(x, axis, [(i, (i + by) % n) for i in range(n)])


def regroup(x):
    return lax.all_to_all(x, SP, split_axis=0, concat_axis=0, tiled=True)


def on_device(queries, keys, values, outputs, out_grad, stats):
    y = lax.axis_index("y")
    xh = lax.axis_index("xh")
    own = regroup(packed_queries(y.reshape(1), queries, out_grad, outputs, stats))
    kv = regroup(packed_keys(keys, values))

    before = shift(own, "y", 1)
    after = shift(own, "y", -1)
    half = NSP // 2
    across = jnp.concatenate([shift(before[:half], "y", 1), shift(after[half:], "y", -1)], axis=0)
    big = jnp.stack([own, before, after, across])
    place = jnp.array([0, 2, 3, 1], jnp.int32)
    where = place[(jnp.arange(NY, dtype=jnp.int32) - y) % NY]

    small = big[:, :, 2 * SHARE : 2 * SHARE + 2, :].astype(F32)
    small = small[..., 0:SHARE] + small[..., SHARE : 2 * SHARE] + small[..., 2 * SHARE : 3 * SHARE]
    small = jnp.take(small.reshape(NY, NY * NX, 4, 2, SHARE), where, axis=0)
    small = jnp.transpose(small, (3, 1, 0, 2, 4)).reshape(2, NY * NX, 1, QB)
    st = small[0] * LOG2E
    de = small[1]

    def table(dy, order):
        base = ((y + dy) % NY) * NX
        ks = jnp.stack([base + (xh + o) % NX for o in order])
        return jnp.concatenate([ks, where]).astype(jnp.int32)

    far, dk, dv = grads_call(2, True, False, BF16, table(2, (1, 0)), big, st, de, kv, ())
    far = shift(far, "y", 2)
    up, dk, dv = grads_call(2, False, False, BF16, table(1, (1, 0)), big, st, de, kv, (dk, dv))
    up = shift(up, "y", 1)
    down, dk, dv = grads_call(2, False, False, BF16, table(-1, (1, 0)), big, st, de, kv, (dk, dv))
    down = shift(down, "y", -1)
    other, dk, dv = grads_call(1, False, False, F32, table(0, (1, 1)), big, st, de, kv, (dk, dv))
    mine, _, _, packed = grads_call(
        1, False, True, F32, table(0, (0, 0)), big, st, de, kv, (dk, dv)
    )
    other = other[0] + (far[0].astype(F32) + up[0].astype(F32) + down[0].astype(F32))
    other = shift(other.astype(BF16), "xh", 1)
    mine = mine[0] + (far[1].astype(F32) + up[1].astype(F32) + down[1].astype(F32))
    mine = (mine + other.astype(F32)) * (ROOT / (KLEN * NY * NX))
    mine = mine.reshape(NSP, QB // NSP, DH).astype(BF16)
    packed = lax.dynamic_update_slice(packed, mine, (0, 2 * KROWS, 0))
    back = jnp.transpose(regroup(packed), (1, 0, 2)).astype(F32).reshape(OUT_ROWS, H * DH)
    return (back[2 * KROWS :], back[:KROWS], back[KROWS : 2 * KROWS])


def solution(mesh):
    torus = Mesh(mesh.devices.reshape(NY, NX, NZ, 2, 2), ALL)
    return jax.shard_map(
        on_device,
        mesh=torus,
        in_specs=(P(SP), P(ALL), P(ALL), P(SP), P(SP), P(SP)),
        out_specs=(P(ALL), P(ALL), P(ALL)),
        check_vma=False,
    )
```

```python
import functools
import math

import jax
import jax.numpy as jnp
from jax import lax
from jax.experimental import pallas as pl
from jax.experimental.pallas import tpu as pltpu
from jax.sharding import Mesh
from jax.sharding import PartitionSpec as P


H = 32
DH = 128
QLEN = 4096
KLEN = 2048
NY, NX, NZ = 4, 2, 8
NKV = NY * NX
SP = ("z", "xl", "c")
ALL = ("y", "xh", "z", "xl", "c")
NSP = 32
ROWS = QLEN // NSP
SHARE = ROWS // NY
GROUP = DH // SHARE
WIDE = 2 * SHARE + 8
KROWS = KLEN // NSP
QB = QLEN // NKV
QROWS = QB // NSP
LOG2E = math.log2(math.e)
ROOT = 1.0 / math.sqrt(DH)
SCALE = 1.0 / (KLEN * NKV)
F32 = jnp.float32
BF16 = jnp.bfloat16


def dot(a, b, dims):
    return lax.dot_general(a, b, ((dims[0], dims[1]), ((), ())), preferred_element_type=F32)


def cost(flops, size, trans=0):
    return pl.CostEstimate(flops=flops, bytes_accessed=size, transcendentals=trans)


def three(x):
    hi = x.astype(BF16).astype(F32)
    mid = (x - hi).astype(BF16).astype(F32)
    return hi, mid, x - hi - mid


def pack_queries(y_ref, group_ref, q_ref, g_ref, o_ref, s_ref, out_ref):
    cols = []
    for h in range(H):
        c = slice(h * DH, (h + 1) * DH)
        out_ref[h, 0:SHARE, :] = q_ref[:, c]
        out_ref[h, SHARE : 2 * SHARE, :] = g_ref[:, c]
        prod = g_ref[:, c].astype(F32) * o_ref[:, c].astype(F32)
        cols.append(jnp.sum(prod, axis=1, keepdims=True))
    delta = jnp.transpose(jnp.concatenate(cols, axis=1))
    stats = s_ref[:, 0:SHARE]
    for b in range(1, NY):
        stats = jnp.where(y_ref[0] == b, s_ref[:, b * SHARE : (b + 1) * SHARE], stats)
    lane = lax.broadcasted_iota(jnp.int32, (H, DH), 1)
    here = lane // SHARE == group_ref[0]
    row = lax.broadcasted_iota(jnp.int32, (H, 8, DH), 1)
    tile = jnp.zeros((H, 8, DH), F32)
    for r, x in enumerate(three(stats * LOG2E) + three(delta)):
        x = jnp.where(here, jnp.concatenate([x] * GROUP, axis=1), 0.0)
        tile = jnp.where(row == r, x[:, None, :], tile)
    out_ref[:, 2 * SHARE : WIDE, :] = tile.astype(BF16)


def packed_queries(y, group, queries, out_grad, outputs, stats):
    wide = pl.BlockSpec((SHARE, H * DH), lambda i, y, g: (y[0], 0))
    return pl.pallas_call(
        pack_queries,
        grid_spec=pltpu.PrefetchScalarGridSpec(
            num_scalar_prefetch=2,
            grid=(1,),
            in_specs=[wide, wide, wide, pl.BlockSpec((H, ROWS), lambda i, y, g: (0, 0))],
            out_specs=pl.BlockSpec((H, WIDE, DH), lambda i, y, g: (0, 0, 0)),
        ),
        out_shape=jax.ShapeDtypeStruct((H, WIDE, DH), BF16),
        cost_estimate=cost(10**6, 2 * 10**6),
        name="pack_queries",
    )(y, group, queries, out_grad, outputs, jnp.transpose(stats))


def pack_keys(k_ref, v_ref, out_ref):
    for h in range(H):
        c = slice(h * DH, (h + 1) * DH)
        out_ref[h, 0:KROWS, :] = k_ref[:, c]
        out_ref[h, KROWS : 2 * KROWS, :] = v_ref[:, c]


def packed_keys(keys, values):
    return pl.pallas_call(
        pack_keys,
        out_shape=jax.ShapeDtypeStruct((H, 2 * KROWS, DH), BF16),
        cost_estimate=cost(10**6, 2 * 10**6),
        name="pack_keys",
    )(keys, values)


def queries_of(parts):
    q = jnp.concatenate([p[:, 0:SHARE, :].reshape(-1, DH) for p in parts], axis=0)
    g = jnp.concatenate([p[:, SHARE : 2 * SHARE, :].reshape(-1, DH) for p in parts], axis=0)
    st, de = [], []
    for p in parts:
        x = jnp.sum(p[:, 2 * SHARE : WIDE, :].astype(F32), axis=0)
        st.append(x[0:1] + x[1:2] + x[2:3])
        de.append(x[3:4] + x[4:5] + x[5:6])
    return q, g, jnp.concatenate(st, axis=1), jnp.concatenate(de, axis=1)


def block_grads(parts, kv_ref, dk_ref, dv_ref, per):
    q, g, st, de = queries_of(parts)
    bk = per * KROWS
    total = None
    for j in range(NSP // per):
        k = kv_ref[j * per : (j + 1) * per, 0:KROWS, :].reshape(bk, DH)
        v = kv_ref[j * per : (j + 1) * per, KROWS : 2 * KROWS, :].reshape(bk, DH)
        at = slice(j * bk, (j + 1) * bk)
        p = jnp.exp2(dot(k, q, ((1,), (1,))) * (ROOT * LOG2E) - st)
        ds = (p * (dot(v, g, ((1,), (1,))) - de)).astype(BF16)
        dv_ref[at, :] += dot(p.astype(BF16), g, ((1,), (0,)))
        dk_ref[at, :] += dot(ds, q, ((1,), (0,)))
        part = dot(ds, k, ((0,), (0,)))
        total = part if total is None else total + part
    return total.reshape(NY, GROUP, SHARE, DH)


def grads(count, first, last, tab, *refs):
    parts = refs[:NY]
    kv_ref = refs[NY]
    rest = refs[NY + 1 :]
    if not first:
        dk_in, dv_in = rest[:2]
        rest = rest[2:]
    dq_refs = rest[:count]
    dk_ref, dv_ref = rest[-2:]
    step = pl.program_id(0)

    @pl.when(step == 0)
    def _():
        dk_ref[...] = jnp.zeros_like(dk_ref) if first else dk_in[...]
        dv_ref[...] = jnp.zeros_like(dv_ref) if first else dv_in[...]

    total = block_grads(parts, kv_ref, dk_ref, dv_ref, 8)
    for n, dq_ref in enumerate(dq_refs):

        @pl.when(step // NX == n)
        def _(dq_ref=dq_ref):
            for b in range(NY):
                dq_ref[0, :, tab[NX * count + b], :, :] = total[b].astype(dq_ref.dtype)

    if last:
        out_ref = rest[count]

        @pl.when(step == NX * count - 1)
        def _():
            dk = (dk_ref[...] * (ROOT * SCALE)).astype(BF16)
            dv = (dv_ref[...] * SCALE).astype(BF16)
            out_ref[:, 0:KROWS, :] = dk.reshape(NSP, KROWS, DH)
            out_ref[:, KROWS : 2 * KROWS, :] = dv.reshape(NSP, KROWS, DH)


DQ = (GROUP, NY, SHARE, DH)
OUT_ROWS = 2 * KROWS + QROWS


def grads_call(count, first, last, tab, parts, kv, sums=()):
    steps = NX * count
    pairs = steps * QB * KLEN

    def dq_spec(n):
        at = lambda i: jnp.clip(i - NX * n, 0, NX - 1)
        return pl.BlockSpec((1, *DQ), lambda i, t: (at(i), 0, 0, 0, 0))

    whole = pl.BlockSpec((KLEN, DH), lambda i, t: (0, 0))
    part = pl.BlockSpec((GROUP, WIDE, DH), lambda i, t: (t[i], 0, 0))
    in_specs = [part] * NY + [pl.BlockSpec((NSP, 2 * KROWS, DH), lambda i, t: (0, 0, 0))]
    out_specs = [dq_spec(n) for n in range(count)]
    out_shape = [jax.ShapeDtypeStruct((NX, *DQ), F32 if last else BF16)] * count
    scratch = []
    if last:
        out_specs.append(pl.BlockSpec((NSP, OUT_ROWS, DH), lambda i, t: (0, 0, 0)))
        out_shape.append(jax.ShapeDtypeStruct((NSP, OUT_ROWS, DH), BF16))
        scratch = [pltpu.VMEM((KLEN, DH), F32)] * 2
    else:
        out_specs += [whole] * 2
        out_shape += [jax.ShapeDtypeStruct((KLEN, DH), F32)] * 2
    return pl.pallas_call(
        functools.partial(grads, count, first, last),
        grid_spec=pltpu.PrefetchScalarGridSpec(
            num_scalar_prefetch=1,
            grid=(steps,),
            in_specs=in_specs + [whole] * len(sums),
            out_specs=out_specs,
            scratch_shapes=scratch,
        ),
        out_shape=out_shape,
        compiler_params=pltpu.CompilerParams(vmem_limit_bytes=26 << 20),
        cost_estimate=cost(pairs * 10 * DH, 4 << 20, pairs),
        name="grads",
    )(tab, *parts, kv, *sums)


def unpack(x_ref, dq_ref, dk_ref, dv_ref):
    for h in range(H):
        c = slice(h * DH, (h + 1) * DH)
        dk_ref[:, c] = x_ref[h, 0:KROWS, :].astype(F32)
        dv_ref[:, c] = x_ref[h, KROWS : 2 * KROWS, :].astype(F32)
        dq_ref[:, c] = x_ref[h, 2 * KROWS : OUT_ROWS, :].astype(F32)


def unpacked(x):
    return pl.pallas_call(
        unpack,
        out_shape=[
            jax.ShapeDtypeStruct((QROWS, H * DH), F32),
            jax.ShapeDtypeStruct((KROWS, H * DH), F32),
            jax.ShapeDtypeStruct((KROWS, H * DH), F32),
        ],
        cost_estimate=cost(10**6, 3 * 10**6),
        name="unpack",
    )(x)


def shift(x, axis, by):
    n = lax.axis_size(axis)
    return lax.ppermute(x, axis, [(i, (i + by) % n) for i in range(n)])


def regroup(x):
    return lax.all_to_all(x, SP, split_axis=0, concat_axis=0, tiled=True)


def body(queries, keys, values, outputs, out_grad, stats):
    y = lax.axis_index("y")
    xh = lax.axis_index("xh")
    group = lax.axis_index("xl") * 2 + lax.axis_index("c")
    at = (y.reshape(1).astype(jnp.int32), group.reshape(1).astype(jnp.int32))
    own = packed_queries(*at, queries, out_grad, outputs, stats)
    own = regroup(own)
    kv = packed_keys(keys, values)
    kv = regroup(kv)

    half = NSP // 2
    before = shift(own, "y", 1)
    after = shift(own, "y", -1)
    low = shift(before[:half], "y", 1)
    high = shift(after[half:], "y", -1)
    parts = (own, before, after, jnp.concatenate([low, high], axis=0))
    where = (y + jnp.array([0, 3, 1, 2], jnp.int32)) % NY

    def members(*dys):
        return [((y + dy) % NY) * NX + (xh + o) % NX for dy in dys for o in (1, 0)]

    def table(ks):
        return jnp.concatenate([jnp.stack(ks), where]).astype(jnp.int32)

    far, up, *sums = grads_call(2, True, False, table(members(2, 1)), parts, kv)
    far = shift(far, "y", 2)
    up = shift(up, "y", 1)
    down, *sums = grads_call(1, False, False, table(members(-1)), parts, kv, sums)
    down = shift(down, "y", -1)
    mine, packed = grads_call(1, False, True, table(members(0)), parts, kv, sums)
    other = mine[0] + (far[0].astype(F32) + up[0].astype(F32) + down[0].astype(F32))
    other = shift(other.astype(BF16), "xh", 1)
    mine = mine[1] + (far[1].astype(F32) + up[1].astype(F32) + down[1].astype(F32))
    mine = (mine + other.astype(F32)) * (ROOT * SCALE)
    mine = mine.reshape(NSP, QROWS, DH).astype(BF16)
    packed = lax.dynamic_update_slice(packed, mine, (0, 2 * KROWS, 0))
    packed = regroup(packed)
    return unpacked(packed)


def solution(mesh):
    torus = Mesh(mesh.devices.reshape(NY, NX, NZ, 2, 2), ALL)
    return jax.shard_map(
        body,
        mesh=torus,
        in_specs=(P(SP), P(ALL), P(ALL), P(SP), P(SP), P(SP)),
        out_specs=(P(ALL), P(ALL), P(ALL)),
        check_vma=False,
    )
```

```python
import functools
import math

import jax
import jax.numpy as jnp
from jax import lax
from jax.experimental import pallas as pl
from jax.experimental.pallas import tpu as pltpu
from jax.sharding import Mesh
from jax.sharding import PartitionSpec as P


H = 32
DH = 128
QLEN = 4096
KLEN = 2048
NY, NX, NZ = 4, 2, 8
NKV = NY * NX
SP = ("z", "xl", "c")
ALL = ("y", "xh", "z", "xl", "c")
NSP = 32
ROWS = QLEN // NSP
SHARE = ROWS // NKV
GROUP = NSP // NKV
LANES = GROUP * SHARE
WIDE = 2 * SHARE + 8
KROWS = KLEN // NSP
QB = QLEN // NKV
QROWS = QB // NSP
LOG2E = math.log2(math.e)
ROOT = 1.0 / math.sqrt(DH)
SCALE = 1.0 / (KLEN * NKV)
F32 = jnp.float32
BF16 = jnp.bfloat16


def dot(a, b, dims):
    return lax.dot_general(a, b, ((dims[0], dims[1]), ((), ())), preferred_element_type=F32)


def cost(flops, size, trans=0):
    return pl.CostEstimate(flops=flops, bytes_accessed=size, transcendentals=trans)


def three(x):
    hi = x.astype(BF16).astype(F32)
    mid = (x - hi).astype(BF16).astype(F32)
    return hi, mid, x - hi - mid


def pack_queries(share_ref, group_ref, q_ref, g_ref, o_ref, s_ref, out_ref):
    cols = []
    for h in range(H):
        c = slice(h * DH, (h + 1) * DH)
        out_ref[h, 0:SHARE, :] = q_ref[:, c]
        out_ref[h, SHARE : 2 * SHARE, :] = g_ref[:, c]
        prod = g_ref[:, c].astype(F32) * o_ref[:, c].astype(F32)
        cols.append(jnp.sum(prod, axis=1, keepdims=True))
    delta = jnp.transpose(jnp.concatenate(cols, axis=1))
    stats = s_ref[:, 0:SHARE]
    for b in range(1, NKV):
        stats = jnp.where(share_ref[0] == b, s_ref[:, b * SHARE : (b + 1) * SHARE], stats)
    lane = lax.broadcasted_iota(jnp.int32, (H, DH), 1)
    here = lane // SHARE % GROUP == group_ref[0]
    row = lax.broadcasted_iota(jnp.int32, (H, 8, DH), 1)
    tile = jnp.zeros((H, 8, DH), F32)
    for r, x in enumerate(three(stats * LOG2E) + three(delta)):
        x = jnp.where(here, jnp.concatenate([x] * (DH // SHARE), axis=1), 0.0)
        tile = jnp.where(row == r, x[:, None, :], tile)
    out_ref[:, 2 * SHARE : WIDE, :] = tile.astype(BF16)


def packed_queries(share, group, queries, out_grad, outputs, stats):
    wide = pl.BlockSpec((SHARE, H * DH), lambda i, y, g: (y[0], 0))
    return pl.pallas_call(
        pack_queries,
        grid_spec=pltpu.PrefetchScalarGridSpec(
            num_scalar_prefetch=2,
            grid=(1,),
            in_specs=[wide, wide, wide, pl.BlockSpec((H, ROWS), lambda i, y, g: (0, 0))],
            out_specs=pl.BlockSpec((H, WIDE, DH), lambda i, y, g: (0, 0, 0)),
        ),
        out_shape=jax.ShapeDtypeStruct((H, WIDE, DH), BF16),
        cost_estimate=cost(10**6, 2 * 10**6),
        name="pack_queries",
    )(share, group, queries, out_grad, outputs, jnp.transpose(stats))


def pack_keys(k_ref, v_ref, out_ref):
    for h in range(H):
        c = slice(h * DH, (h + 1) * DH)
        out_ref[h, 0:KROWS, :] = k_ref[:, c]
        out_ref[h, KROWS : 2 * KROWS, :] = v_ref[:, c]


def packed_keys(keys, values):
    return pl.pallas_call(
        pack_keys,
        out_shape=jax.ShapeDtypeStruct((H, 2 * KROWS, DH), BF16),
        cost_estimate=cost(10**6, 2 * 10**6),
        name="pack_keys",
    )(keys, values)


def queries_of(parts):
    q = jnp.concatenate([p[:, 0:SHARE, :].reshape(-1, DH) for p in parts], axis=0)
    g = jnp.concatenate([p[:, SHARE : 2 * SHARE, :].reshape(-1, DH) for p in parts], axis=0)
    low = lax.broadcasted_iota(jnp.int32, (8, DH), 1) < LANES
    st, de = [], []
    for one, two in zip(parts[0::2], parts[1::2]):
        one = jnp.sum(one[:, 2 * SHARE : WIDE, :].astype(F32), axis=0)
        two = jnp.sum(two[:, 2 * SHARE : WIDE, :].astype(F32), axis=0)
        x = jnp.where(low, one, two)
        st.append(x[0:1] + x[1:2] + x[2:3])
        de.append(x[3:4] + x[4:5] + x[5:6])
    return q, g, jnp.concatenate(st, axis=1), jnp.concatenate(de, axis=1)


def block_grads(parts, kv_ref, dk_ref, dv_ref, per):
    q, g, st, de = queries_of(parts)
    bk = per * KROWS
    total = None
    for j in range(NSP // per):
        k = kv_ref[j * per : (j + 1) * per, 0:KROWS, :].reshape(bk, DH)
        v = kv_ref[j * per : (j + 1) * per, KROWS : 2 * KROWS, :].reshape(bk, DH)
        at = slice(j * bk, (j + 1) * bk)
        p = jnp.exp2(dot(k, q, ((1,), (1,))) * (ROOT * LOG2E) - st)
        ds = (p * (dot(v, g, ((1,), (1,))) - de)).astype(BF16)
        dv_ref[at, :] += dot(p.astype(BF16), g, ((1,), (0,)))
        dk_ref[at, :] += dot(ds, q, ((1,), (0,)))
        part = dot(ds, k, ((0,), (0,)))
        total = part if total is None else total + part
    return total.reshape(NKV, GROUP, SHARE, DH)


def grads(count, first, last, tab, *refs):
    parts = refs[:NKV]
    kv_ref = refs[NKV]
    rest = refs[NKV + 1 :]
    if not first:
        dk_in, dv_in = rest[:2]
        rest = rest[2:]
    dq_refs = rest[:count]
    dk_ref, dv_ref = rest[-2:]
    step = pl.program_id(0)

    @pl.when(step == 0)
    def _():
        dk_ref[...] = jnp.zeros_like(dk_ref) if first else dk_in[...]
        dv_ref[...] = jnp.zeros_like(dv_ref) if first else dv_in[...]

    total = block_grads(parts, kv_ref, dk_ref, dv_ref, 8)
    for n, dq_ref in enumerate(dq_refs):

        @pl.when(step // NX == n)
        def _(dq_ref=dq_ref):
            for b in range(NKV):
                dq_ref[0, :, tab[NX * count + b], :, :] = total[b].astype(dq_ref.dtype)

    if last:
        out_ref = rest[count]

        @pl.when(step == NX * count - 1)
        def _():
            dk = (dk_ref[...] * (ROOT * SCALE)).astype(BF16)
            dv = (dv_ref[...] * SCALE).astype(BF16)
            out_ref[:, 0:KROWS, :] = dk.reshape(NSP, KROWS, DH)
            out_ref[:, KROWS : 2 * KROWS, :] = dv.reshape(NSP, KROWS, DH)


DQ = (GROUP, NKV, SHARE, DH)
OUT_ROWS = 2 * KROWS + QROWS


def grads_call(count, first, last, tab, parts, kv, sums=()):
    steps = NX * count
    pairs = steps * QB * KLEN

    def dq_spec(n):
        at = lambda i: jnp.clip(i - NX * n, 0, NX - 1)
        return pl.BlockSpec((1, *DQ), lambda i, t: (at(i), 0, 0, 0, 0))

    whole = pl.BlockSpec((KLEN, DH), lambda i, t: (0, 0))
    part = pl.BlockSpec((GROUP, WIDE, DH), lambda i, t: (t[i], 0, 0))
    in_specs = [part] * NKV + [pl.BlockSpec((NSP, 2 * KROWS, DH), lambda i, t: (0, 0, 0))]
    out_specs = [dq_spec(n) for n in range(count)]
    out_shape = [jax.ShapeDtypeStruct((NX, *DQ), F32 if last else BF16)] * count
    scratch = []
    if last:
        out_specs.append(pl.BlockSpec((NSP, OUT_ROWS, DH), lambda i, t: (0, 0, 0)))
        out_shape.append(jax.ShapeDtypeStruct((NSP, OUT_ROWS, DH), BF16))
        scratch = [pltpu.VMEM((KLEN, DH), F32)] * 2
    else:
        out_specs += [whole] * 2
        out_shape += [jax.ShapeDtypeStruct((KLEN, DH), F32)] * 2
    return pl.pallas_call(
        functools.partial(grads, count, first, last),
        grid_spec=pltpu.PrefetchScalarGridSpec(
            num_scalar_prefetch=1,
            grid=(steps,),
            in_specs=in_specs + [whole] * len(sums),
            out_specs=out_specs,
            scratch_shapes=scratch,
        ),
        out_shape=out_shape,
        compiler_params=pltpu.CompilerParams(vmem_limit_bytes=26 << 20),
        cost_estimate=cost(pairs * 10 * DH, 4 << 20, pairs),
        name="grads",
    )(tab, *parts, kv, *sums)


def unpack(x_ref, dq_ref, dk_ref, dv_ref):
    for h in range(x_ref.shape[0]):
        c = slice(h * DH, (h + 1) * DH)
        dk_ref[:, c] = x_ref[h, 0:KROWS, :].astype(F32)
        dv_ref[:, c] = x_ref[h, KROWS : 2 * KROWS, :].astype(F32)
        dq_ref[:, c] = x_ref[h, 2 * KROWS : OUT_ROWS, :].astype(F32)


def unpacked(x):
    steps = 4

    def wide(rows):
        return pl.BlockSpec((rows, H * DH // steps), lambda i: (0, i))

    return pl.pallas_call(
        unpack,
        grid=(steps,),
        in_specs=[pl.BlockSpec((H // steps, OUT_ROWS, DH), lambda i: (i, 0, 0))],
        out_specs=[wide(QROWS), wide(KROWS), wide(KROWS)],
        out_shape=[
            jax.ShapeDtypeStruct((QROWS, H * DH), F32),
            jax.ShapeDtypeStruct((KROWS, H * DH), F32),
            jax.ShapeDtypeStruct((KROWS, H * DH), F32),
        ],
        cost_estimate=cost(10**6, 3 * 10**6),
        name="unpack",
    )(x)


def shift(x, axis, by):
    n = lax.axis_size(axis)
    return lax.ppermute(x, axis, [(i, (i + by) % n) for i in range(n)])


def regroup(x):
    return lax.all_to_all(x, SP, split_axis=0, concat_axis=0, tiled=True)


def body(queries, keys, values, outputs, out_grad, stats):
    y = lax.axis_index("y")
    xh = lax.axis_index("xh")
    group = lax.axis_index("xl") * 2 + lax.axis_index("c")
    share = (y * NX + xh).astype(jnp.int32)
    at = (share.reshape(1), group.reshape(1).astype(jnp.int32))
    own = packed_queries(*at, queries, out_grad, outputs, stats)
    own = regroup(own)
    kv = packed_keys(keys, values)
    kv = regroup(kv)

    before = shift(own, "y", 1)
    after = shift(own, "y", -1)
    own2 = shift(own, "xh", 1)
    before2 = shift(own2, "y", 1)
    after2 = shift(own2, "y", -1)
    across = shift(before, "y", 1)
    across2 = shift(after2, "y", -1)
    parts = (own, own2, before, before2, after, after2, across, across2)
    away = (y + jnp.array([0, 0, 3, 3, 1, 1, 2, 2], jnp.int32)) % NY
    where = away * NX + (xh + jnp.array([0, 1] * NY, jnp.int32)) % NX

    def members(*dys):
        return [((y + dy) % NY) * NX + (xh + o) % NX for dy in dys for o in (1, 0)]

    def table(ks):
        return jnp.concatenate([jnp.stack(ks), where]).astype(jnp.int32)

    far, up, *sums = grads_call(2, True, False, table(members(2, 1)), parts, kv)
    far = shift(far, "y", 2)
    up = shift(up, "y", 1)
    down, *sums = grads_call(1, False, False, table(members(-1)), parts, kv, sums)
    down = shift(down, "y", -1)
    mine, packed = grads_call(1, False, True, table(members(0)), parts, kv, sums)
    other = mine[0] + (far[0].astype(F32) + up[0].astype(F32) + down[0].astype(F32))
    other = shift(other.astype(BF16), "xh", 1)
    mine = mine[1] + (far[1].astype(F32) + up[1].astype(F32) + down[1].astype(F32))
    mine = (mine + other.astype(F32)) * (ROOT * SCALE)
    mine = mine.reshape(NSP, QROWS, DH).astype(BF16)
    packed = lax.dynamic_update_slice(packed, mine, (0, 2 * KROWS, 0))
    packed = regroup(packed)
    return unpacked(packed)


def solution(mesh):
    torus = Mesh(mesh.devices.reshape(NY, NX, NZ, 2, 2), ALL)
    return jax.shard_map(
        body,
        mesh=torus,
        in_specs=(P(SP), P(ALL), P(ALL), P(SP), P(SP), P(SP)),
        out_specs=(P(ALL), P(ALL), P(ALL)),
        check_vma=False,
    )
```

```python
import functools
import math

import jax
import jax.numpy as jnp
from jax import lax
from jax.experimental import pallas as pl
from jax.experimental.pallas import tpu as pltpu
from jax.sharding import Mesh
from jax.sharding import PartitionSpec as P


H = 32
DH = 128
QLEN = 4096
KLEN = 2048
NY, NX, NZ = 4, 2, 8
NKV = NY * NX
SP = ("z", "xl", "c")
ALL = ("y", "xh", "z", "xl", "c")
NSP = 32
ROWS = QLEN // NSP
SHARE = ROWS // NY
GROUP = DH // SHARE
WIDE = 2 * SHARE
KROWS = KLEN // NSP
KWIDE = 2 * KROWS + 8
QB = QLEN // NKV
QROWS = QB // NSP
LOG2E = math.log2(math.e)
ROOT = 1.0 / math.sqrt(DH)
SCALE = 1.0 / (KLEN * NKV)
F32 = jnp.float32
BF16 = jnp.bfloat16


def dot(a, b, dims):
    return lax.dot_general(a, b, ((dims[0], dims[1]), ((), ())), preferred_element_type=F32)


def cost(flops, size, trans=0):
    return pl.CostEstimate(flops=flops, bytes_accessed=size, transcendentals=trans)


def three(x):
    hi = x.astype(BF16).astype(F32)
    mid = (x - hi).astype(BF16).astype(F32)
    return hi, mid, x - hi - mid


def pack_queries(y_ref, q_ref, g_ref, out_ref):
    for h in range(H):
        c = slice(h * DH, (h + 1) * DH)
        out_ref[h, 0:SHARE, :] = q_ref[:, c]
        out_ref[h, SHARE:WIDE, :] = g_ref[:, c]


def packed_queries(y, queries, out_grad):
    wide = pl.BlockSpec((SHARE, H * DH), lambda i, y: (y[0], 0))
    return pl.pallas_call(
        pack_queries,
        grid_spec=pltpu.PrefetchScalarGridSpec(
            num_scalar_prefetch=1,
            grid=(1,),
            in_specs=[wide, wide],
            out_specs=pl.BlockSpec((H, WIDE, DH), lambda i, y: (0, 0, 0)),
        ),
        out_shape=jax.ShapeDtypeStruct((H, WIDE, DH), BF16),
        cost_estimate=cost(10**6, 10**6),
        name="pack_queries",
    )(y, queries, out_grad)


def pack_keys(y_ref, k_ref, v_ref, g_ref, o_ref, s_ref, out_ref):
    cols = []
    for h in range(H):
        c = slice(h * DH, (h + 1) * DH)
        out_ref[h, 0:KROWS, :] = k_ref[:, c]
        out_ref[h, KROWS : 2 * KROWS, :] = v_ref[:, c]
        prod = g_ref[:, c].astype(F32) * o_ref[:, c].astype(F32)
        cols.append(jnp.sum(prod, axis=1, keepdims=True))
    delta = jnp.transpose(jnp.concatenate(cols, axis=1))
    row = lax.broadcasted_iota(jnp.int32, (H, 8, DH), 1)
    tile = jnp.zeros((H, 8, DH), F32)
    for r, x in enumerate(three(s_ref[...] * LOG2E) + three(delta)):
        turned = x
        for b in range(1, NY):
            at = b * SHARE
            turned = jnp.where(
                y_ref[0] == b, jnp.concatenate([x[:, at:], x[:, :at]], axis=1), turned
            )
        tile = jnp.where(row == r, turned[:, None, :], tile)
    out_ref[:, 2 * KROWS : KWIDE, :] = tile.astype(BF16)


def packed_keys(y, keys, values, out_grad, outputs, stats):
    def whole(*shape):
        return pl.BlockSpec(shape, lambda i, y: (0,) * len(shape))

    return pl.pallas_call(
        pack_keys,
        grid_spec=pltpu.PrefetchScalarGridSpec(
            num_scalar_prefetch=1,
            grid=(1,),
            in_specs=[whole(KROWS, H * DH)] * 2 + [whole(ROWS, H * DH)] * 2 + [whole(H, ROWS)],
            out_specs=whole(H, KWIDE, DH),
        ),
        out_shape=jax.ShapeDtypeStruct((H, KWIDE, DH), BF16),
        cost_estimate=cost(10**6, 4 * 10**6),
        name="pack_keys",
    )(y, keys, values, out_grad, outputs, jnp.transpose(stats))


def in_lanes(x):
    return jnp.concatenate(
        [
            x[s : s + 1, b * SHARE : (b + 1) * SHARE]
            for b in range(NY)
            for s in range(GROUP)
        ],
        axis=1,
    )


def queries_of(member, refs, kv_ref):
    own, after, low, high, before = refs
    far = jnp.where(member < NKV // 2, low[...], high[...])
    parts = (own[...], after[...], far, before[...])
    q = jnp.concatenate([p[:, 0:SHARE, :].reshape(-1, DH) for p in parts], axis=0)
    g = jnp.concatenate([p[:, SHARE:WIDE, :].reshape(-1, DH) for p in parts], axis=0)
    tile = kv_ref[pl.ds(member * GROUP, GROUP), 2 * KROWS : KWIDE, :].astype(F32)
    st = tile[:, 0, :] + tile[:, 1, :] + tile[:, 2, :]
    de = tile[:, 3, :] + tile[:, 4, :] + tile[:, 5, :]
    return q, g, in_lanes(st), in_lanes(de)


def block_grads(member, parts, kv_ref, dk_ref, dv_ref, per):
    q, g, st, de = queries_of(member, parts, kv_ref)
    bk = per * KROWS
    total = None
    for j in range(NSP // per):
        k = kv_ref[j * per : (j + 1) * per, 0:KROWS, :].reshape(bk, DH)
        v = kv_ref[j * per : (j + 1) * per, KROWS : 2 * KROWS, :].reshape(bk, DH)
        at = slice(j * bk, (j + 1) * bk)
        p = jnp.exp2(dot(k, q, ((1,), (1,))) * (ROOT * LOG2E) - st)
        ds = (p * (dot(v, g, ((1,), (1,))) - de)).astype(BF16)
        dv_ref[at, :] += dot(p.astype(BF16), g, ((1,), (0,)))
        dk_ref[at, :] += dot(ds, q, ((1,), (0,)))
        part = dot(ds, k, ((0,), (0,)))
        total = part if total is None else total + part
    return total.reshape(NY, GROUP, SHARE, DH)


def grads(count, first, last, tab, *refs):
    parts = refs[: NY + 1]
    kv_ref = refs[NY + 1]
    rest = refs[NY + 2 :]
    if not first:
        dk_in, dv_in = rest[:2]
        rest = rest[2:]
    dq_refs = rest[:count]
    dk_ref, dv_ref = rest[-2:]
    step = pl.program_id(0)

    @pl.when(step == 0)
    def _():
        dk_ref[...] = jnp.zeros_like(dk_ref) if first else dk_in[...]
        dv_ref[...] = jnp.zeros_like(dv_ref) if first else dv_in[...]

    total = block_grads(tab[step], parts, kv_ref, dk_ref, dv_ref, 8)
    for n, dq_ref in enumerate(dq_refs):

        @pl.when(step // NX == n)
        def _(dq_ref=dq_ref):
            for b in range(NY):
                dq_ref[0, :, tab[NX * count + b], :, :] = total[b].astype(dq_ref.dtype)

    if last:
        out_ref = rest[count]

        @pl.when(step == NX * count - 1)
        def _():
            dk = (dk_ref[...] * (ROOT * SCALE)).astype(BF16)
            dv = (dv_ref[...] * SCALE).astype(BF16)
            out_ref[:, 0:KROWS, :] = dk.reshape(NSP, KROWS, DH)
            out_ref[:, KROWS : 2 * KROWS, :] = dv.reshape(NSP, KROWS, DH)


DQ = (GROUP, NY, SHARE, DH)
OUT_ROWS = 2 * KROWS + QROWS


def grads_call(count, first, last, tab, parts, kv, sums=()):
    steps = NX * count
    pairs = steps * QB * KLEN

    def dq_spec(n):
        at = lambda i: jnp.clip(i - NX * n, 0, NX - 1)
        return pl.BlockSpec((1, *DQ), lambda i, t: (at(i), 0, 0, 0, 0))

    whole = pl.BlockSpec((KLEN, DH), lambda i, t: (0, 0))
    part = pl.BlockSpec((GROUP, WIDE, DH), lambda i, t: (t[i], 0, 0))
    half = NKV // 2
    low = pl.BlockSpec(part.block_shape, lambda i, t: (jnp.minimum(t[i], half - 1), 0, 0))
    high = pl.BlockSpec(part.block_shape, lambda i, t: (jnp.maximum(t[i] - half, 0), 0, 0))
    in_specs = [part, part, low, high, part]
    in_specs.append(pl.BlockSpec((NSP, KWIDE, DH), lambda i, t: (0, 0, 0)))
    out_specs = [dq_spec(n) for n in range(count)]
    out_shape = [jax.ShapeDtypeStruct((NX, *DQ), F32 if last else BF16)] * count
    scratch = []
    if last:
        out_specs.append(pl.BlockSpec((NSP, OUT_ROWS, DH), lambda i, t: (0, 0, 0)))
        out_shape.append(jax.ShapeDtypeStruct((NSP, OUT_ROWS, DH), BF16))
        scratch = [pltpu.VMEM((KLEN, DH), F32)] * 2
    else:
        out_specs += [whole] * 2
        out_shape += [jax.ShapeDtypeStruct((KLEN, DH), F32)] * 2
    return pl.pallas_call(
        functools.partial(grads, count, first, last),
        grid_spec=pltpu.PrefetchScalarGridSpec(
            num_scalar_prefetch=1,
            grid=(steps,),
            in_specs=in_specs + [whole] * len(sums),
            out_specs=out_specs,
            scratch_shapes=scratch,
        ),
        out_shape=out_shape,
        compiler_params=pltpu.CompilerParams(vmem_limit_bytes=26 << 20),
        cost_estimate=cost(pairs * 10 * DH, 4 << 20, pairs),
        name="grads",
    )(tab, *parts, kv, *sums)


def unpack(x_ref, *refs):
    outs, bufs, sems = refs[:3], refs[3:6], refs[6]
    copies = []
    pieces = [(0, 0, QROWS, 2 * KROWS)]
    for n in (1, 2):
        for r in range(0, KROWS, KROWS // 2):
            pieces.append((n, r, KROWS // 2, (n - 1) * KROWS + r))
    for p, (n, r, rows, at) in enumerate(pieces):
        for h in range(H):
            bufs[n][r : r + rows, h * DH : (h + 1) * DH] = x_ref[h, at : at + rows, :].astype(F32)
        copy = pltpu.make_async_copy(
            bufs[n].at[r : r + rows], outs[n].at[r : r + rows], sems.at[p]
        )
        copy.start()
        copies.append(copy)
    for copy in copies:
        copy.wait()


def unpacked(x):
    shapes = [(QROWS, H * DH), (KROWS, H * DH), (KROWS, H * DH)]
    return pl.pallas_call(
        unpack,
        in_specs=[pl.BlockSpec(memory_space=pltpu.VMEM)],
        out_specs=[pl.BlockSpec(memory_space=pl.ANY)] * 3,
        out_shape=[jax.ShapeDtypeStruct(shape, F32) for shape in shapes],
        scratch_shapes=[pltpu.VMEM(shape, F32) for shape in shapes]
        + [pltpu.SemaphoreType.DMA((5,))],
        cost_estimate=cost(10**6, 3 * 10**6),
        name="unpack",
    )(x)


def shift(x, axis, by):
    n = lax.axis_size(axis)
    return lax.ppermute(x, axis, [(i, (i + by) % n) for i in range(n)])


def regroup(x):
    return lax.all_to_all(x, SP, split_axis=0, concat_axis=0, tiled=True)


def body(queries, keys, values, outputs, out_grad, stats):
    y = lax.axis_index("y")
    xh = lax.axis_index("xh")
    at = y.reshape(1).astype(jnp.int32)
    own = packed_queries(at, queries, out_grad)
    own = regroup(own)
    kv = packed_keys(at, keys, values, out_grad, outputs, stats)
    kv = regroup(kv)

    half = NSP // 2
    before = shift(own, "y", 1)
    after = shift(own, "y", -1)
    low = shift(before[:half], "y", 1)
    high = shift(after[half:], "y", -1)
    parts = (own, after, low, high, before)
    where = (y + jnp.arange(NY, dtype=jnp.int32)) % NY

    def members(*dys):
        return [((y + dy) % NY) * NX + (xh + o) % NX for dy in dys for o in (1, 0)]

    def table(ks):
        return jnp.concatenate([jnp.stack(ks), where]).astype(jnp.int32)

    far, up, *sums = grads_call(2, True, False, table(members(2, 1)), parts, kv)
    far = shift(far, "y", 2)
    up = shift(up, "y", 1)
    down, *sums = grads_call(1, False, False, table(members(-1)), parts, kv, sums)
    down = shift(down, "y", -1)
    mine, packed = grads_call(1, False, True, table(members(0)), parts, kv, sums)
    other = mine[0] + (far[0].astype(F32) + up[0].astype(F32) + down[0].astype(F32))
    other = shift(other.astype(BF16), "xh", 1)
    mine = mine[1] + (far[1].astype(F32) + up[1].astype(F32) + down[1].astype(F32))
    mine = (mine + other.astype(F32)) * (ROOT * SCALE)
    mine = mine.reshape(NSP, QROWS, DH).astype(BF16)
    packed = lax.dynamic_update_slice(packed, mine, (0, 2 * KROWS, 0))
    packed = regroup(packed)
    return unpacked(packed)


def solution(mesh):
    torus = Mesh(mesh.devices.reshape(NY, NX, NZ, 2, 2), ALL)
    return jax.shard_map(
        body,
        mesh=torus,
        in_specs=(P(SP), P(ALL), P(ALL), P(SP), P(SP), P(SP)),
        out_specs=(P(ALL), P(ALL), P(ALL)),
        check_vma=False,
    )
```

```python
import functools
import math

import jax
import jax.numpy as jnp
from jax import lax
from jax.experimental import pallas as pl
from jax.experimental.pallas import tpu as pltpu
from jax.sharding import Mesh
from jax.sharding import PartitionSpec as P


H = 32
DH = 128
QLEN = 4096
KLEN = 2048
NY, NX, NZ = 4, 2, 8
NKV = NY * NX
SP = ("z", "xl", "c")
TURN = ("xl", "c", "z")
ALL = ("y", "xh", "z", "xl", "c")
NSP = 32
ROWS = QLEN // NSP
SHARE = ROWS // NY
GROUP = DH // SHARE
WIDE = 2 * SHARE
KROWS = KLEN // NSP
KWIDE = 2 * KROWS + 8
QB = QLEN // NKV
QROWS = QB // NSP
LOG2E = math.log2(math.e)
ROOT = 1.0 / math.sqrt(DH)
SCALE = 1.0 / (KLEN * NKV)
F32 = jnp.float32
BF16 = jnp.bfloat16


def dot(a, b, dims):
    return lax.dot_general(a, b, ((dims[0], dims[1]), ((), ())), preferred_element_type=F32)


def cost(flops, size, trans=0):
    return pl.CostEstimate(flops=flops, bytes_accessed=size, transcendentals=trans)


def three(x):
    hi = x.astype(BF16).astype(F32)
    mid = (x - hi).astype(BF16).astype(F32)
    return hi, mid, x - hi - mid


def pack_queries(y_ref, q_ref, g_ref, out_ref):
    for h in range(H):
        c = slice(h * DH, (h + 1) * DH)
        out_ref[h, 0:SHARE, :] = q_ref[:, c]
        out_ref[h, SHARE:WIDE, :] = g_ref[:, c]


def packed_queries(y, queries, out_grad):
    wide = pl.BlockSpec((SHARE, H * DH), lambda i, y: (y[0], 0))
    return pl.pallas_call(
        pack_queries,
        grid_spec=pltpu.PrefetchScalarGridSpec(
            num_scalar_prefetch=1,
            grid=(1,),
            in_specs=[wide, wide],
            out_specs=pl.BlockSpec((H, WIDE, DH), lambda i, y: (0, 0, 0)),
        ),
        out_shape=jax.ShapeDtypeStruct((H, WIDE, DH), BF16),
        cost_estimate=cost(10**6, 10**6),
        name="pack_queries",
    )(y, queries, out_grad)


def pack_keys(y_ref, k_ref, v_ref, g_ref, o_ref, s_ref, out_ref):
    cols = []
    for h in range(H):
        c = slice(h * DH, (h + 1) * DH)
        out_ref[h, 0:KROWS, :] = k_ref[:, c]
        out_ref[h, KROWS : 2 * KROWS, :] = v_ref[:, c]
        prod = g_ref[:, c].astype(F32) * o_ref[:, c].astype(F32)
        cols.append(jnp.sum(prod, axis=1, keepdims=True))
    delta = jnp.transpose(jnp.concatenate(cols, axis=1))
    row = lax.broadcasted_iota(jnp.int32, (H, 8, DH), 1)
    tile = jnp.zeros((H, 8, DH), F32)
    for r, x in enumerate(three(s_ref[...] * LOG2E) + three(delta)):
        turned = x
        for b in range(1, NY):
            at = b * SHARE
            turned = jnp.where(
                y_ref[0] == b, jnp.concatenate([x[:, at:], x[:, :at]], axis=1), turned
            )
        tile = jnp.where(row == r, turned[:, None, :], tile)
    out_ref[:, 2 * KROWS : KWIDE, :] = tile.astype(BF16)


def packed_keys(y, keys, values, out_grad, outputs, stats):
    def whole(*shape):
        return pl.BlockSpec(shape, lambda i, y: (0,) * len(shape))

    return pl.pallas_call(
        pack_keys,
        grid_spec=pltpu.PrefetchScalarGridSpec(
            num_scalar_prefetch=1,
            grid=(1,),
            in_specs=[whole(KROWS, H * DH)] * 2 + [whole(ROWS, H * DH)] * 2 + [whole(H, ROWS)],
            out_specs=whole(H, KWIDE, DH),
        ),
        out_shape=jax.ShapeDtypeStruct((H, KWIDE, DH), BF16),
        cost_estimate=cost(10**6, 4 * 10**6),
        name="pack_keys",
    )(y, keys, values, out_grad, outputs, jnp.transpose(stats))


def in_lanes(x):
    return jnp.concatenate(
        [
            x[s : s + 1, b * SHARE : (b + 1) * SHARE]
            for b in range(NY)
            for s in range(GROUP)
        ],
        axis=1,
    )


def queries_of(member, refs, kv_ref):
    own, after, low, high, before = refs
    far = jnp.concatenate([low[...], high[...]], axis=0)
    parts = (own[...], after[...], far, before[...])
    q = jnp.concatenate([p[:, 0, 0:SHARE, :].reshape(-1, DH) for p in parts], axis=0)
    g = jnp.concatenate([p[:, 0, SHARE:WIDE, :].reshape(-1, DH) for p in parts], axis=0)
    tile = kv_ref[:, member, 2 * KROWS : KWIDE, :].astype(F32)
    st = tile[:, 0, :] + tile[:, 1, :] + tile[:, 2, :]
    de = tile[:, 3, :] + tile[:, 4, :] + tile[:, 5, :]
    return q, g, in_lanes(st), in_lanes(de)


def block_grads(member, parts, kv_ref, dk_ref, dv_ref):
    q, g, st, de = queries_of(member, parts, kv_ref)
    bk = NKV * KROWS
    total = None
    for j in range(GROUP):
        k = kv_ref[j, :, 0:KROWS, :].reshape(bk, DH)
        v = kv_ref[j, :, KROWS : 2 * KROWS, :].reshape(bk, DH)
        at = slice(j * bk, (j + 1) * bk)
        p = jnp.exp2(dot(k, q, ((1,), (1,))) * (ROOT * LOG2E) - st)
        ds = (p * (dot(v, g, ((1,), (1,))) - de)).astype(BF16)
        dv_ref[at, :] += dot(p.astype(BF16), g, ((1,), (0,)))
        dk_ref[at, :] += dot(ds, q, ((1,), (0,)))
        part = dot(ds, k, ((0,), (0,)))
        total = part if total is None else total + part
    return total.reshape(NY, GROUP, SHARE, DH)


def grads(count, first, last, tab, *refs):
    parts = refs[: NY + 1]
    kv_ref = refs[NY + 1]
    rest = refs[NY + 2 :]
    if not first:
        dk_in, dv_in = rest[:2]
        rest = rest[2:]
    dq_refs = rest[:count]
    dk_ref, dv_ref = rest[-2:]
    step = pl.program_id(0)

    @pl.when(step == 0)
    def _():
        dk_ref[...] = jnp.zeros_like(dk_ref) if first else dk_in[...]
        dv_ref[...] = jnp.zeros_like(dv_ref) if first else dv_in[...]

    total = block_grads(tab[step], parts, kv_ref, dk_ref, dv_ref)
    for n, dq_ref in enumerate(dq_refs):

        @pl.when(step // NX == n)
        def _(dq_ref=dq_ref):
            for b in range(NY):
                dq_ref[0, :, tab[NX * count + b], :, :] = total[b].astype(dq_ref.dtype)

    if last:
        out_ref = rest[count]

        @pl.when(step == NX * count - 1)
        def _():
            dk = (dk_ref[...] * (ROOT * SCALE)).astype(BF16)
            dv = (dv_ref[...] * SCALE).astype(BF16)
            out_ref[:, 0:KROWS, :] = dk.reshape(NSP, KROWS, DH)
            out_ref[:, KROWS : 2 * KROWS, :] = dv.reshape(NSP, KROWS, DH)


DQ = (GROUP, NY, SHARE, DH)
OUT_ROWS = 2 * KROWS + QROWS


def grads_call(count, first, last, tab, parts, kv, sums=()):
    steps = NX * count
    pairs = steps * QB * KLEN

    def dq_spec(n):
        at = lambda i: jnp.clip(i - NX * n, 0, NX - 1)
        return pl.BlockSpec((1, *DQ), lambda i, t: (at(i), 0, 0, 0, 0))

    whole = pl.BlockSpec((KLEN, DH), lambda i, t: (0, 0))
    part = pl.BlockSpec((GROUP, 1, WIDE, DH), lambda i, t: (0, t[i], 0, 0))
    half = pl.BlockSpec((GROUP // 2, 1, WIDE, DH), lambda i, t: (0, t[i], 0, 0))
    in_specs = [part, part, half, half, part]
    in_specs.append(pl.BlockSpec((GROUP, NKV, KWIDE, DH), lambda i, t: (0, 0, 0, 0)))
    out_specs = [dq_spec(n) for n in range(count)]
    out_shape = [jax.ShapeDtypeStruct((NX, *DQ), F32 if last else BF16)] * count
    scratch = []
    if last:
        out_specs.append(pl.BlockSpec((NSP, OUT_ROWS, DH), lambda i, t: (0, 0, 0)))
        out_shape.append(jax.ShapeDtypeStruct((NSP, OUT_ROWS, DH), BF16))
        scratch = [pltpu.VMEM((KLEN, DH), F32)] * 2
    else:
        out_specs += [whole] * 2
        out_shape += [jax.ShapeDtypeStruct((KLEN, DH), F32)] * 2
    return pl.pallas_call(
        functools.partial(grads, count, first, last),
        grid_spec=pltpu.PrefetchScalarGridSpec(
            num_scalar_prefetch=1,
            grid=(steps,),
            in_specs=in_specs + [whole] * len(sums),
            out_specs=out_specs,
            scratch_shapes=scratch,
        ),
        out_shape=out_shape,
        compiler_params=pltpu.CompilerParams(vmem_limit_bytes=26 << 20),
        cost_estimate=cost(pairs * 10 * DH, 4 << 20, pairs),
        name="grads",
    )(tab, *parts, kv, *sums)


def unpack(x_ref, *refs):
    outs, bufs, sems = refs[:3], refs[3:6], refs[6]
    copies = []
    pieces = [(0, 0, QROWS, 2 * KROWS)]
    for n in (1, 2):
        for r in range(0, KROWS, KROWS // 2):
            pieces.append((n, r, KROWS // 2, (n - 1) * KROWS + r))
    for p, (n, r, rows, at) in enumerate(pieces):
        for h in range(H):
            bufs[n][r : r + rows, h * DH : (h + 1) * DH] = x_ref[h, at : at + rows, :].astype(F32)
        copy = pltpu.make_async_copy(
            bufs[n].at[r : r + rows], outs[n].at[r : r + rows], sems.at[p]
        )
        copy.start()
        copies.append(copy)
    for copy in copies:
        copy.wait()


def unpacked(x):
    shapes = [(QROWS, H * DH), (KROWS, H * DH), (KROWS, H * DH)]
    return pl.pallas_call(
        unpack,
        in_specs=[pl.BlockSpec(memory_space=pltpu.VMEM)],
        out_specs=[pl.BlockSpec(memory_space=pl.ANY)] * 3,
        out_shape=[jax.ShapeDtypeStruct(shape, F32) for shape in shapes],
        scratch_shapes=[pltpu.VMEM(shape, F32) for shape in shapes]
        + [pltpu.SemaphoreType.DMA((5,))],
        compiler_params=pltpu.CompilerParams(vmem_limit_bytes=8 << 20),
        cost_estimate=cost(10**6, 3 * 10**6),
        name="unpack",
    )(x)


def shift(x, axis, by):
    n = lax.axis_size(axis)
    return lax.ppermute(x, axis, [(i, (i + by) % n) for i in range(n)])


def regroup(x):
    return lax.all_to_all(x, TURN, split_axis=0, concat_axis=0, tiled=True)


def by_z(x):
    return x.reshape(-1, NZ, *x.shape[1:])


def body(queries, keys, values, outputs, out_grad, stats):
    y = lax.axis_index("y")
    xh = lax.axis_index("xh")
    at = y.reshape(1).astype(jnp.int32)
    own = packed_queries(at, queries, out_grad)
    own = regroup(own)
    kv = packed_keys(at, keys, values, out_grad, outputs, stats)
    kv = regroup(kv)

    half = NSP // 2
    before = shift(own, "y", 1)
    after = shift(own, "y", -1)
    low = shift(before[:half], "y", 1)
    high = shift(after[half:], "y", -1)
    parts = [by_z(x) for x in (own, after, low, high, before)]
    kv = by_z(kv)
    where = (y + jnp.arange(NY, dtype=jnp.int32)) % NY

    def members(*dys):
        return [((y + dy) % NY) * NX + (xh + o) % NX for dy in dys for o in (1, 0)]

    def table(ks):
        return jnp.concatenate([jnp.stack(ks), where]).astype(jnp.int32)

    far, up, *sums = grads_call(2, True, False, table(members(2, 1)), parts, kv)
    far = shift(far, "y", 2)
    up = shift(up, "y", 1)
    down, *sums = grads_call(1, False, False, table(members(-1)), parts, kv, sums)
    down = shift(down, "y", -1)
    mine, packed = grads_call(1, False, True, table(members(0)), parts, kv, sums)
    other = mine[0] + (far[0].astype(F32) + up[0].astype(F32) + down[0].astype(F32))
    other = shift(other.astype(BF16), "xh", 1)
    mine = mine[1] + (far[1].astype(F32) + up[1].astype(F32) + down[1].astype(F32))
    mine = (mine + other.astype(F32)) * (ROOT * SCALE)
    mine = jnp.swapaxes(mine.reshape(NZ, NSP // NZ, QROWS, DH), 0, 1)
    mine = mine.reshape(NSP, QROWS, DH).astype(BF16)
    packed = lax.dynamic_update_slice(packed, mine, (0, 2 * KROWS, 0))
    packed = regroup(packed)
    return unpacked(packed)


def solution(mesh):
    torus = Mesh(mesh.devices.reshape(NY, NX, NZ, 2, 2), ALL)
    return jax.shard_map(
        body,
        mesh=torus,
        in_specs=(P(SP), P(ALL), P(ALL), P(SP), P(SP), P(SP)),
        out_specs=(P(ALL), P(ALL), P(ALL)),
        check_vma=False,
    )
```

```python
import functools
import math

import jax
import jax.numpy as jnp
from jax import lax
from jax.experimental import pallas as pl
from jax.experimental.pallas import tpu as pltpu
from jax.sharding import Mesh
from jax.sharding import PartitionSpec as P


H = 32
DH = 128
QLEN = 4096
KLEN = 2048
NY, NX, NZ = 4, 2, 8
NKV = NY * NX
SP = ("z", "xl", "c")
ALL = ("y", "xh", "z", "xl", "c")
PLANE = ("xl", "c", "y", "xh")
NSP = 32
NXC = 4
ROWS = QLEN // NSP
SHARE = ROWS // NKV
WIDE = 2 * SHARE
TALL = WIDE + 8
KROWS = KLEN // NSP
QB = QLEN // NZ
PART = QB // NZ
QROWS = QB // NSP
LOG2E = math.log2(math.e)
ROOT = 1.0 / math.sqrt(DH)
SCALE = 1.0 / (KLEN * NKV)
F32 = jnp.float32
BF16 = jnp.bfloat16


def dot(a, b, dims):
    return lax.dot_general(a, b, ((dims[0], dims[1]), ((), ())), preferred_element_type=F32)


def cost(flops, size, trans=0):
    return pl.CostEstimate(flops=flops, bytes_accessed=size, transcendentals=trans)


def three(x):
    hi = x.astype(BF16).astype(F32)
    mid = (x - hi).astype(BF16).astype(F32)
    return hi, mid, x - hi - mid


def pack_queries(b_ref, q_ref, g_ref, o_ref, s_ref, out_ref):
    cols = []
    for h in range(H):
        c = slice(h * DH, (h + 1) * DH)
        out_ref[h, 0:SHARE, :] = q_ref[:, c]
        out_ref[h, SHARE:WIDE, :] = g_ref[:, c]
        prod = g_ref[:, c].astype(F32) * o_ref[:, c].astype(F32)
        cols.append(jnp.sum(prod, axis=1, keepdims=True))
    delta = jnp.transpose(jnp.concatenate(cols, axis=1))
    lane = lax.broadcasted_iota(jnp.int32, (H, DH), 1)
    here = lane // SHARE == b_ref[0]
    row = lax.broadcasted_iota(jnp.int32, (H, 8, DH), 1)
    tile = jnp.zeros((H, 8, DH), F32)
    delta = jnp.concatenate([delta] * NKV, axis=1)
    for r, x in enumerate(three(s_ref[...] * LOG2E) + three(delta)):
        x = jnp.where(here, x, 0.0)
        tile = jnp.where(row == r, x[:, None, :], tile)
    out_ref[:, WIDE:TALL, :] = tile.astype(BF16)


def packed_queries(b, queries, out_grad, outputs, stats):
    wide = pl.BlockSpec((SHARE, H * DH), lambda i, b: (b[0], 0))
    return pl.pallas_call(
        pack_queries,
        grid_spec=pltpu.PrefetchScalarGridSpec(
            num_scalar_prefetch=1,
            grid=(1,),
            in_specs=[wide, wide, wide, pl.BlockSpec((H, ROWS), lambda i, b: (0, 0))],
            out_specs=pl.BlockSpec((H, TALL, DH), lambda i, b: (0, 0, 0)),
        ),
        out_shape=jax.ShapeDtypeStruct((H, TALL, DH), BF16),
        cost_estimate=cost(10**6, 10**6),
        name="pack_queries",
    )(b, queries, out_grad, outputs, jnp.transpose(stats))


def gather_stats(x_ref, out_ref):
    out_ref[0:NSP] = x_ref[:, 0:WIDE, :]
    tile = x_ref[:, WIDE:TALL, :].astype(F32).reshape(NXC, NKV, 8, DH)
    out_ref[NSP] = jnp.sum(tile, axis=1).reshape(WIDE, DH).astype(BF16)


def with_stats(x):
    return pl.pallas_call(
        gather_stats,
        out_shape=jax.ShapeDtypeStruct((NSP + 1, WIDE, DH), BF16),
        compiler_params=pltpu.CompilerParams(vmem_limit_bytes=8 << 20),
        cost_estimate=cost(10**6, 10**6),
        name="gather_stats",
    )(x)


def pack_keys(k_ref, v_ref, out_ref):
    for h in range(H):
        c = slice(h * DH, (h + 1) * DH)
        out_ref[h, 0:KROWS, :] = k_ref[:, c]
        out_ref[h, KROWS : 2 * KROWS, :] = v_ref[:, c]


def packed_keys(keys, values):
    return pl.pallas_call(
        pack_keys,
        out_shape=jax.ShapeDtypeStruct((H, 2 * KROWS, DH), BF16),
        cost_estimate=cost(10**6, 2 * 10**6),
        name="pack_keys",
    )(keys, values)


def queries_of(to_z, parts, tiles):
    q = jnp.concatenate([p[:, 0:SHARE, :].reshape(PART, DH) for p in parts], axis=0)
    g = jnp.concatenate([p[:, SHARE:WIDE, :].reshape(PART, DH) for p in parts], axis=0)
    st, de = [], []
    for tile in tiles:
        x = tile[0].astype(F32)
        x = jnp.where(to_z % 2 == 0, x[:, :PART], x[:, PART:])
        st.append(x[0:1] + x[1:2] + x[2:3])
        de.append(x[3:4] + x[4:5] + x[5:6])
    return q, g, jnp.concatenate(st, axis=1), jnp.concatenate(de, axis=1)


def block_grads(to_z, parts, tiles, kv_ref, dk_ref, dv_ref):
    q, g, st, de = queries_of(to_z, parts, tiles)
    per = 8
    bk = per * KROWS
    total = None
    for j in range(NSP // per):
        k = kv_ref[j * per : (j + 1) * per, 0:KROWS, :].reshape(bk, DH)
        v = kv_ref[j * per : (j + 1) * per, KROWS : 2 * KROWS, :].reshape(bk, DH)
        at = slice(j * bk, (j + 1) * bk)
        p = jnp.exp2(dot(k, q, ((1,), (1,))) * (ROOT * LOG2E) - st)
        ds = (p * (dot(v, g, ((1,), (1,))) - de)).astype(BF16)
        dv_ref[at, :] += dot(p.astype(BF16), g, ((1,), (0,)))
        dk_ref[at, :] += dot(ds, q, ((1,), (0,)))
        part = dot(ds, k, ((0,), (0,)))
        total = part if total is None else total + part
    return total.reshape(NZ, PART, DH)


def grads(count, first, last, tab, *refs):
    parts = refs[:NZ]
    tiles = refs[NZ : 2 * NZ]
    kv_ref = refs[2 * NZ]
    rest = refs[2 * NZ + 1 :]
    if not first:
        dk_in, dv_in = rest[:2]
        rest = rest[2:]
    dq_refs = rest[:count]
    dk_ref, dv_ref = rest[-2:]
    step = pl.program_id(0)

    @pl.when(step == 0)
    def _():
        dk_ref[...] = jnp.zeros_like(dk_ref) if first else dk_in[...]
        dv_ref[...] = jnp.zeros_like(dv_ref) if first else dv_in[...]

    total = block_grads(tab[step], parts, tiles, kv_ref, dk_ref, dv_ref)
    for n, dq_ref in enumerate(dq_refs):

        @pl.when(step == n)
        def _(dq_ref=dq_ref):
            for j in range(NZ):
                dq_ref[tab[count + j]] = total[j].astype(dq_ref.dtype)

    if last:
        out_ref = rest[count]

        @pl.when(step == count - 1)
        def _():
            dk = (dk_ref[...] * (ROOT * SCALE)).astype(BF16)
            dv = (dv_ref[...] * SCALE).astype(BF16)
            out_ref[:, 0:KROWS, :] = dk.reshape(NSP, KROWS, DH)
            out_ref[:, KROWS : 2 * KROWS, :] = dv.reshape(NSP, KROWS, DH)


OUT_ROWS = 2 * KROWS + QROWS


def grads_call(count, first, last, tab, parts, kv, sums=()):
    pairs = count * QB * KLEN
    whole = pl.BlockSpec((KLEN, DH), lambda i, t: (0, 0))
    part = pl.BlockSpec((PART // SHARE, WIDE, DH), lambda i, t: (t[i], 0, 0))
    tile = pl.BlockSpec((1, 8, DH), lambda i, t: (NSP, t[i] // 2, 0))
    in_specs = [part] * NZ + [tile] * NZ
    in_specs.append(pl.BlockSpec((NSP, 2 * KROWS, DH), lambda i, t: (0, 0, 0)))
    out_specs = [pl.BlockSpec((NZ, PART, DH), lambda i, t: (0, 0, 0))] * count
    out_shape = [jax.ShapeDtypeStruct((NZ, PART, DH), F32 if last else BF16)] * count
    scratch = []
    if last:
        out_specs.append(pl.BlockSpec((NSP, OUT_ROWS, DH), lambda i, t: (0, 0, 0)))
        out_shape.append(jax.ShapeDtypeStruct((NSP, OUT_ROWS, DH), BF16))
        scratch = [pltpu.VMEM((KLEN, DH), F32)] * 2
    else:
        out_specs += [whole] * 2
        out_shape += [jax.ShapeDtypeStruct((KLEN, DH), F32)] * 2
    return pl.pallas_call(
        functools.partial(grads, count, first, last),
        grid_spec=pltpu.PrefetchScalarGridSpec(
            num_scalar_prefetch=1,
            grid=(count,),
            in_specs=in_specs + [whole] * len(sums),
            out_specs=out_specs,
            scratch_shapes=scratch,
        ),
        out_shape=out_shape,
        compiler_params=pltpu.CompilerParams(vmem_limit_bytes=26 << 20),
        cost_estimate=cost(pairs * 10 * DH, 4 << 20, pairs),
        name="grads",
    )(tab, *parts, *parts, kv, *sums)


def unpack(x_ref, *refs):
    outs, bufs, sems = refs[:3], refs[3:6], refs[6]
    copies = []
    pieces = [(0, 0, QROWS, 2 * KROWS)]
    for n in (1, 2):
        for r in range(0, KROWS, KROWS // 2):
            pieces.append((n, r, KROWS // 2, (n - 1) * KROWS + r))
    for p, (n, r, rows, at) in enumerate(pieces):
        for h in range(H):
            bufs[n][r : r + rows, h * DH : (h + 1) * DH] = x_ref[h, at : at + rows, :].astype(F32)
        copy = pltpu.make_async_copy(
            bufs[n].at[r : r + rows], outs[n].at[r : r + rows], sems.at[p]
        )
        copy.start()
        copies.append(copy)
    for copy in copies:
        copy.wait()


def unpacked(x):
    shapes = [(QROWS, H * DH), (KROWS, H * DH), (KROWS, H * DH)]
    return pl.pallas_call(
        unpack,
        in_specs=[pl.BlockSpec(memory_space=pltpu.VMEM)],
        out_specs=[pl.BlockSpec(memory_space=pl.ANY)] * 3,
        out_shape=[jax.ShapeDtypeStruct(shape, F32) for shape in shapes],
        scratch_shapes=[pltpu.VMEM(shape, F32) for shape in shapes]
        + [pltpu.SemaphoreType.DMA((5,))],
        compiler_params=pltpu.CompilerParams(vmem_limit_bytes=8 << 20),
        cost_estimate=cost(10**6, 3 * 10**6),
        name="unpack",
    )(x)


def shift(x, axis, by):
    n = lax.axis_size(axis)
    return lax.ppermute(x, axis, [(i, (i + by) % n) for i in range(n)])


def regroup(x):
    return lax.all_to_all(x, PLANE, split_axis=0, concat_axis=0, tiled=True)


def body(queries, keys, values, outputs, out_grad, stats):
    z = lax.axis_index("z")
    b = lax.axis_index(("y", "xh")).astype(jnp.int32).reshape(1)
    own = packed_queries(b, queries, out_grad, outputs, stats)
    own = regroup(own)
    kv = packed_keys(keys, values)
    kv = regroup(kv)
    own = with_stats(own)

    up, down = [own], [own]
    for n in range(1, NZ // 2 + 1):
        up.append(shift(up[-1], "z", 1))
        if n < NZ // 2:
            down.append(shift(down[-1], "z", -1))
    parts = up[::-1] + down[1:]
    half = NZ // 2
    where = (z + jnp.arange(-half, half, dtype=jnp.int32)) % NZ

    sent = []
    sums = ()
    groups = ((4, 3, -3), (2, -2), (1, -1), (0,))
    for n, group in enumerate(groups):
        tab = jnp.concatenate([(z + jnp.array(group, jnp.int32)) % NZ, where])
        first, last = n == 0, n == len(groups) - 1
        out = grads_call(
            len(group), first, last, tab.astype(jnp.int32), parts, kv, sums
        )
        sums = out[len(group) :]
        for by, dq in zip(group, out):
            if by:
                sent.append(shift(dq, "z", by))
            else:
                mine = dq
    mine = mine + sum(x.astype(F32) for x in sent)
    mine = (mine * (ROOT * SCALE)).reshape(NKV, NXC, QROWS, DH)
    mine = jnp.swapaxes(mine, 0, 1).reshape(NSP, QROWS, DH).astype(BF16)
    packed = lax.dynamic_update_slice(sums[0], mine, (0, 2 * KROWS, 0))
    packed = regroup(packed)
    return unpacked(packed)


def solution(mesh):
    torus = Mesh(mesh.devices.reshape(NY, NX, NZ, 2, 2), ALL)
    return jax.shard_map(
        body,
        mesh=torus,
        in_specs=(P(SP), P(ALL), P(ALL), P(SP), P(SP), P(SP)),
        out_specs=(P(ALL), P(ALL), P(ALL)),
        check_vma=False,
    )
```

```python
import functools
import math

import jax
import jax.numpy as jnp
from jax import lax
from jax.experimental import pallas as pl
from jax.experimental.pallas import tpu as pltpu
from jax.sharding import Mesh
from jax.sharding import PartitionSpec as P


H = 32
DH = 128
QLEN = 4096
KLEN = 2048
NY, NX, NZ = 4, 2, 8
NKV = NY * NX
SP = ("z", "xl", "c")
ALL = ("y", "xh", "z", "xl", "c")
PLANE = ("xl", "c", "y", "xh")
NSP = 32
NXC = 4
ROWS = QLEN // NSP
SHARE = ROWS // NKV
WIDE = 2 * SHARE
TALL = WIDE + 8
KROWS = KLEN // NSP
QB = QLEN // NZ
PART = QB // NZ
QROWS = QB // NSP
LOG2E = math.log2(math.e)
ROOT = 1.0 / math.sqrt(DH)
SCALE = 1.0 / (KLEN * NKV)
F32 = jnp.float32
BF16 = jnp.bfloat16


def dot(a, b, dims):
    return lax.dot_general(a, b, ((dims[0], dims[1]), ((), ())), preferred_element_type=F32)


def cost(flops, size, trans=0):
    return pl.CostEstimate(flops=flops, bytes_accessed=size, transcendentals=trans)


def three(x):
    hi = x.astype(BF16).astype(F32)
    mid = (x - hi).astype(BF16).astype(F32)
    return hi, mid, x - hi - mid


def pack_queries(b_ref, q_ref, g_ref, o_ref, s_ref, out_ref):
    cols = []
    for h in range(H):
        c = slice(h * DH, (h + 1) * DH)
        out_ref[h, 0:SHARE, :] = q_ref[:, c]
        out_ref[h, SHARE:WIDE, :] = g_ref[:, c]
        prod = g_ref[:, c].astype(F32) * o_ref[:, c].astype(F32)
        cols.append(jnp.sum(prod, axis=1, keepdims=True))
    delta = jnp.transpose(jnp.concatenate(cols, axis=1))
    lane = lax.broadcasted_iota(jnp.int32, (H, DH), 1)
    here = lane // SHARE == b_ref[0]
    row = lax.broadcasted_iota(jnp.int32, (H, 8, DH), 1)
    tile = jnp.zeros((H, 8, DH), F32)
    delta = jnp.concatenate([delta] * NKV, axis=1)
    for r, x in enumerate(three(s_ref[...] * LOG2E) + three(delta)):
        x = jnp.where(here, x, 0.0)
        tile = jnp.where(row == r, x[:, None, :], tile)
    out_ref[:, WIDE:TALL, :] = tile.astype(BF16)


def packed_queries(b, queries, out_grad, outputs, stats):
    wide = pl.BlockSpec((SHARE, H * DH), lambda i, b: (b[0], 0))
    return pl.pallas_call(
        pack_queries,
        grid_spec=pltpu.PrefetchScalarGridSpec(
            num_scalar_prefetch=1,
            grid=(1,),
            in_specs=[wide, wide, wide, pl.BlockSpec((H, ROWS), lambda i, b: (0, 0))],
            out_specs=pl.BlockSpec((H, TALL, DH), lambda i, b: (0, 0, 0)),
        ),
        out_shape=jax.ShapeDtypeStruct((H, TALL, DH), BF16),
        cost_estimate=cost(10**6, 10**6),
        name="pack_queries",
    )(b, queries, out_grad, outputs, jnp.transpose(stats))


def gather_stats(x_ref, out_ref):
    out_ref[0:NSP] = x_ref[:, 0:WIDE, :]
    tile = x_ref[:, WIDE:TALL, :].astype(F32).reshape(NXC, NKV, 8, DH)
    out_ref[NSP] = jnp.sum(tile, axis=1).reshape(WIDE, DH).astype(BF16)


def with_stats(x):
    return pl.pallas_call(
        gather_stats,
        out_shape=jax.ShapeDtypeStruct((NSP + 1, WIDE, DH), BF16),
        compiler_params=pltpu.CompilerParams(vmem_limit_bytes=8 << 20),
        cost_estimate=cost(10**6, 10**6),
        name="gather_stats",
    )(x)


def pack_keys(k_ref, v_ref, out_ref):
    for h in range(H):
        c = slice(h * DH, (h + 1) * DH)
        out_ref[h, 0:KROWS, :] = k_ref[:, c]
        out_ref[h, KROWS : 2 * KROWS, :] = v_ref[:, c]


def packed_keys(keys, values):
    return pl.pallas_call(
        pack_keys,
        out_shape=jax.ShapeDtypeStruct((H, 2 * KROWS, DH), BF16),
        cost_estimate=cost(10**6, 2 * 10**6),
        name="pack_keys",
    )(keys, values)


def queries_of(to_z, parts, tiles):
    q = jnp.concatenate([p[:, 0:SHARE, :].reshape(PART, DH) for p in parts], axis=0)
    g = jnp.concatenate([p[:, SHARE:WIDE, :].reshape(PART, DH) for p in parts], axis=0)
    st, de = [], []
    for tile in tiles:
        x = tile[0].astype(F32)
        x = jnp.where(to_z % 2 == 0, x[:, :PART], x[:, PART:])
        st.append(x[0:1] + x[1:2] + x[2:3])
        de.append(x[3:4] + x[4:5] + x[5:6])
    return q, g, jnp.concatenate(st, axis=1), jnp.concatenate(de, axis=1)


def block_grads(to_z, parts, tiles, kv_ref, dk_ref, dv_ref):
    q, g, st, de = queries_of(to_z, parts, tiles)
    per = 8
    bk = per * KROWS
    total = None
    for j in range(NSP // per):
        k = kv_ref[j * per : (j + 1) * per, 0:KROWS, :].reshape(bk, DH)
        v = kv_ref[j * per : (j + 1) * per, KROWS : 2 * KROWS, :].reshape(bk, DH)
        at = slice(j * bk, (j + 1) * bk)
        p = jnp.exp2(dot(k, q, ((1,), (1,))) * (ROOT * LOG2E) - st)
        ds = (p * (dot(v, g, ((1,), (1,))) - de)).astype(BF16)
        dv_ref[at, :] += dot(p.astype(BF16), g, ((1,), (0,)))
        dk_ref[at, :] += dot(ds, q, ((1,), (0,)))
        part = dot(ds, k, ((0,), (0,)))
        total = part if total is None else total + part
    return total.reshape(NZ, PART, DH)


def grads(count, first, last, tab, *refs):
    parts = refs[:NZ]
    tiles = refs[NZ : 2 * NZ]
    kv_ref = refs[2 * NZ]
    rest = refs[2 * NZ + 1 :]
    if not first:
        dk_in, dv_in = rest[:2]
        rest = rest[2:]
    dq_refs = rest[:count]
    dk_ref, dv_ref = rest[-2:]
    step = pl.program_id(0)

    @pl.when(step == 0)
    def _():
        dk_ref[...] = jnp.zeros_like(dk_ref) if first else dk_in[...]
        dv_ref[...] = jnp.zeros_like(dv_ref) if first else dv_in[...]

    total = block_grads(tab[step], parts, tiles, kv_ref, dk_ref, dv_ref)
    for n, dq_ref in enumerate(dq_refs):

        @pl.when(step == n)
        def _(dq_ref=dq_ref):
            for j in range(NZ):
                dq_ref[tab[count + j]] = total[j].astype(dq_ref.dtype)

    if last:
        out_ref = rest[count]

        @pl.when(step == count - 1)
        def _():
            dk = (dk_ref[...] * (ROOT * SCALE)).astype(BF16)
            dv = (dv_ref[...] * SCALE).astype(BF16)
            out_ref[:, 0:KROWS, :] = dk.reshape(NSP, KROWS, DH)
            out_ref[:, KROWS : 2 * KROWS, :] = dv.reshape(NSP, KROWS, DH)


OUT_ROWS = 2 * KROWS + QROWS


def grads_call(count, first, last, tab, parts, kv, sums=()):
    pairs = count * QB * KLEN
    whole = pl.BlockSpec((KLEN, DH), lambda i, t: (0, 0))
    part = pl.BlockSpec((PART // SHARE, WIDE, DH), lambda i, t: (t[i], 0, 0))
    tile = pl.BlockSpec((1, 8, DH), lambda i, t: (NSP, t[i] // 2, 0))
    in_specs = [part] * NZ + [tile] * NZ
    in_specs.append(pl.BlockSpec((NSP, 2 * KROWS, DH), lambda i, t: (0, 0, 0)))
    out_specs = [pl.BlockSpec((NZ, PART, DH), lambda i, t: (0, 0, 0))] * count
    out_shape = [jax.ShapeDtypeStruct((NZ, PART, DH), F32 if last else BF16)] * count
    scratch = []
    if last:
        out_specs.append(pl.BlockSpec((NSP, OUT_ROWS, DH), lambda i, t: (0, 0, 0)))
        out_shape.append(jax.ShapeDtypeStruct((NSP, OUT_ROWS, DH), BF16))
        scratch = [pltpu.VMEM((KLEN, DH), F32)] * 2
    else:
        out_specs += [whole] * 2
        out_shape += [jax.ShapeDtypeStruct((KLEN, DH), F32)] * 2
    return pl.pallas_call(
        functools.partial(grads, count, first, last),
        grid_spec=pltpu.PrefetchScalarGridSpec(
            num_scalar_prefetch=1,
            grid=(count,),
            in_specs=in_specs + [whole] * len(sums),
            out_specs=out_specs,
            scratch_shapes=scratch,
        ),
        out_shape=out_shape,
        compiler_params=pltpu.CompilerParams(vmem_limit_bytes=26 << 20),
        cost_estimate=cost(pairs * 10 * DH, 4 << 20, pairs),
        name="grads",
    )(tab, *parts, *parts, kv, *sums)


def unpack(x_ref, *refs):
    outs, bufs, sems = refs[:3], refs[3:6], refs[6]
    copies = []
    pieces = [(0, 0, QROWS, 2 * KROWS)]
    for n in (1, 2):
        for r in range(0, KROWS, KROWS // 2):
            pieces.append((n, r, KROWS // 2, (n - 1) * KROWS + r))
    for p, (n, r, rows, at) in enumerate(pieces):
        for h in range(H):
            bufs[n][r : r + rows, h * DH : (h + 1) * DH] = x_ref[h, at : at + rows, :].astype(F32)
        copy = pltpu.make_async_copy(
            bufs[n].at[r : r + rows], outs[n].at[r : r + rows], sems.at[p]
        )
        copy.start()
        copies.append(copy)
    for copy in copies:
        copy.wait()


def unpacked(x):
    shapes = [(QROWS, H * DH), (KROWS, H * DH), (KROWS, H * DH)]
    return pl.pallas_call(
        unpack,
        in_specs=[pl.BlockSpec(memory_space=pltpu.VMEM)],
        out_specs=[pl.BlockSpec(memory_space=pl.ANY)] * 3,
        out_shape=[jax.ShapeDtypeStruct(shape, F32) for shape in shapes],
        scratch_shapes=[pltpu.VMEM(shape, F32) for shape in shapes]
        + [pltpu.SemaphoreType.DMA((5,))],
        compiler_params=pltpu.CompilerParams(vmem_limit_bytes=8 << 20),
        cost_estimate=cost(10**6, 3 * 10**6),
        name="unpack",
    )(x)


def turn(x, by):
    pairs = []
    for z in range(NZ):
        for c in range(2):
            pairs.append((z * 2 + c, (z + (1 - 2 * c) * by) % NZ * 2 + c))
    return lax.ppermute(x, ("z", "c"), pairs)


def regroup(x):
    return lax.all_to_all(x, PLANE, split_axis=0, concat_axis=0, tiled=True)


def body(queries, keys, values, outputs, out_grad, stats):
    z = lax.axis_index("z")
    b = lax.axis_index(("y", "xh")).astype(jnp.int32).reshape(1)
    own = packed_queries(b, queries, out_grad, outputs, stats)
    own = regroup(own)
    kv = packed_keys(keys, values)
    kv = regroup(kv)
    own = with_stats(own)

    one, two = [own], [own]
    for n in range(1, NZ // 2 + 1):
        one.append(turn(one[-1], 1))
        if n < NZ // 2:
            two.append(turn(two[-1], -1))
    parts = one[::-1] + two[1:]
    half = NZ // 2
    sign = 1 - 2 * lax.axis_index("c")
    where = (z + sign * jnp.arange(-half, half, dtype=jnp.int32)) % NZ

    sent = []
    sums = ()
    groups = ((4, 3, -3), (2, -2), (1, -1), (0,))
    for n, group in enumerate(groups):
        tab = jnp.concatenate([(z + sign * jnp.array(group, jnp.int32)) % NZ, where])
        first, last = n == 0, n == len(groups) - 1
        out = grads_call(
            len(group), first, last, tab.astype(jnp.int32), parts, kv, sums
        )
        sums = out[len(group) :]
        for by, dq in zip(group, out):
            if by:
                sent.append(turn(dq, by))
            else:
                mine = dq
    mine = mine + sum(x.astype(F32) for x in sent)
    mine = (mine * (ROOT * SCALE)).reshape(NKV, NXC, QROWS, DH)
    mine = jnp.swapaxes(mine, 0, 1).reshape(NSP, QROWS, DH).astype(BF16)
    packed = lax.dynamic_update_slice(sums[0], mine, (0, 2 * KROWS, 0))
    packed = regroup(packed)
    return unpacked(packed)


def solution(mesh):
    torus = Mesh(mesh.devices.reshape(NY, NX, NZ, 2, 2), ALL)
    return jax.shard_map(
        body,
        mesh=torus,
        in_specs=(P(SP), P(ALL), P(ALL), P(SP), P(SP), P(SP)),
        out_specs=(P(ALL), P(ALL), P(ALL)),
        check_vma=False,
    )
```

```python
import functools
import math

import jax
import jax.numpy as jnp
from jax import lax
from jax.experimental import pallas as pl
from jax.experimental.pallas import tpu as pltpu
from jax.sharding import Mesh
from jax.sharding import PartitionSpec as P


H = 32
DH = 128
QLEN = 4096
KLEN = 2048
NY, NX, NZ = 4, 2, 8
NKV = NY * NX
SP = ("z", "xl", "c")
ALL = ("y", "xh", "z", "xl", "c")
PLANE = ("xl", "c", "y", "xh")
NSP = 32
NXC = 4
ROWS = QLEN // NSP
SHARE = ROWS // NKV
WIDE = 2 * SHARE
TALL = WIDE + 8
KROWS = KLEN // NSP
QB = QLEN // NZ
PART = QB // NZ
QROWS = QB // NSP
LOG2E = math.log2(math.e)
ROOT = 1.0 / math.sqrt(DH)
SCALE = 1.0 / (KLEN * NKV)
F32 = jnp.float32
BF16 = jnp.bfloat16


def dot(a, b, dims):
    return lax.dot_general(a, b, ((dims[0], dims[1]), ((), ())), preferred_element_type=F32)


def cost(flops, size, trans=0):
    return pl.CostEstimate(flops=flops, bytes_accessed=size, transcendentals=trans)


def three(x):
    hi = x.astype(BF16).astype(F32)
    mid = (x - hi).astype(BF16).astype(F32)
    return hi, mid, x - hi - mid


def pack_queries(b_ref, q_ref, g_ref, o_ref, s_ref, out_ref):
    cols = []
    for h in range(H):
        c = slice(h * DH, (h + 1) * DH)
        out_ref[h, 0:SHARE, :] = q_ref[:, c]
        out_ref[h, SHARE:WIDE, :] = g_ref[:, c]
        prod = g_ref[:, c].astype(F32) * o_ref[:, c].astype(F32)
        cols.append(jnp.sum(prod, axis=1, keepdims=True))
    delta = jnp.transpose(jnp.concatenate(cols, axis=1))
    lane = lax.broadcasted_iota(jnp.int32, (H, DH), 1)
    here = lane // SHARE == b_ref[0]
    row = lax.broadcasted_iota(jnp.int32, (H, 8, DH), 1)
    tile = jnp.zeros((H, 8, DH), F32)
    delta = jnp.concatenate([delta] * NKV, axis=1)
    for r, x in enumerate(three(s_ref[...] * LOG2E) + three(delta)):
        x = jnp.where(here, x, 0.0)
        tile = jnp.where(row == r, x[:, None, :], tile)
    out_ref[:, WIDE:TALL, :] = tile.astype(BF16)


def packed_queries(b, queries, out_grad, outputs, stats):
    wide = pl.BlockSpec((SHARE, H * DH), lambda i, b: (b[0], 0))
    return pl.pallas_call(
        pack_queries,
        grid_spec=pltpu.PrefetchScalarGridSpec(
            num_scalar_prefetch=1,
            grid=(1,),
            in_specs=[wide, wide, wide, pl.BlockSpec((H, ROWS), lambda i, b: (0, 0))],
            out_specs=pl.BlockSpec((H, TALL, DH), lambda i, b: (0, 0, 0)),
        ),
        out_shape=jax.ShapeDtypeStruct((H, TALL, DH), BF16),
        cost_estimate=cost(10**6, 10**6),
        name="pack_queries",
    )(b, queries, out_grad, outputs, jnp.transpose(stats))


def gather_stats(x_ref, out_ref):
    out_ref[0:NSP] = x_ref[:, 0:WIDE, :]
    tile = x_ref[:, WIDE:TALL, :].astype(F32).reshape(NXC, NKV, 8, DH)
    out_ref[NSP] = jnp.sum(tile, axis=1).reshape(WIDE, DH).astype(BF16)


def with_stats(x):
    return pl.pallas_call(
        gather_stats,
        out_shape=jax.ShapeDtypeStruct((NSP + 1, WIDE, DH), BF16),
        compiler_params=pltpu.CompilerParams(vmem_limit_bytes=8 << 20),
        cost_estimate=cost(10**6, 10**6),
        name="gather_stats",
    )(x)


def pack_keys(k_ref, v_ref, out_ref):
    for h in range(H):
        c = slice(h * DH, (h + 1) * DH)
        out_ref[h, 0:KROWS, :] = k_ref[:, c]
        out_ref[h, KROWS : 2 * KROWS, :] = v_ref[:, c]


def packed_keys(keys, values):
    return pl.pallas_call(
        pack_keys,
        out_shape=jax.ShapeDtypeStruct((H, 2 * KROWS, DH), BF16),
        cost_estimate=cost(10**6, 2 * 10**6),
        name="pack_keys",
    )(keys, values)


def queries_of(to_z, parts, tiles):
    q = jnp.concatenate([p[:, 0:SHARE, :].reshape(PART, DH) for p in parts], axis=0)
    g = jnp.concatenate([p[:, SHARE:WIDE, :].reshape(PART, DH) for p in parts], axis=0)
    st, de = [], []
    for tile in tiles:
        x = tile[0].astype(F32)
        x = jnp.where(to_z % 2 == 0, x[:, :PART], x[:, PART:])
        st.append(x[0:1] + x[1:2] + x[2:3])
        de.append(x[3:4] + x[4:5] + x[5:6])
    return q, g, jnp.concatenate(st, axis=1), jnp.concatenate(de, axis=1)


def block_grads(to_z, parts, tiles, kv_ref, dk_ref, dv_ref, total_ref):
    q, g, st, de = queries_of(to_z, parts, tiles)
    per = 8
    bk = per * KROWS

    def one(j):
        sources = pl.ds(pl.multiple_of(j * per, per), per)
        k = kv_ref[sources, 0:KROWS, :].reshape(bk, DH)
        v = kv_ref[sources, KROWS : 2 * KROWS, :].reshape(bk, DH)
        at = pl.ds(pl.multiple_of(j * bk, bk), bk)
        p = jnp.exp2(dot(k, q, ((1,), (1,))) * (ROOT * LOG2E) - st)
        ds = (p * (dot(v, g, ((1,), (1,))) - de)).astype(BF16)
        dv_ref[at, :] += dot(p.astype(BF16), g, ((1,), (0,)))
        dk_ref[at, :] += dot(ds, q, ((1,), (0,)))
        return dot(ds, k, ((0,), (0,)))

    total_ref[...] = jnp.zeros_like(total_ref)

    def some(i, nothing):
        parts = [one(i * UNROLL + j) for j in range(UNROLL)]
        total_ref[...] += functools.reduce(jnp.add, parts)
        return nothing

    lax.fori_loop(0, NSP // per // UNROLL, some, 0)
    return total_ref[...].reshape(NZ, PART, DH)


def grads(first, added, last, tab, *refs):
    parts = refs[:NZ]
    tiles = refs[NZ : 2 * NZ]
    kv_ref = refs[2 * NZ]
    rest, total_ref = refs[2 * NZ + 1 : -1], refs[-1]
    if not first:
        dk_in, dv_in = rest[:2]
        rest = rest[2:]
    if added:
        sum_ref = rest[0]
        rest = rest[1:]
    dq_ref = rest[0]
    dk_ref, dv_ref = rest[-2:]
    dk_ref[...] = jnp.zeros_like(dk_ref) if first else dk_in[...]
    dv_ref[...] = jnp.zeros_like(dv_ref) if first else dv_in[...]
    total = block_grads(tab[0], parts, tiles, kv_ref, dk_ref, dv_ref, total_ref)
    for j in range(NZ):
        at = tab[1 + j]
        part = total[j]
        if added:
            part = part + sum_ref[at].astype(F32)
        dq_ref[at] = part.astype(dq_ref.dtype)
    if last:
        out_ref = rest[1]
        dk = (dk_ref[...] * (ROOT * SCALE)).astype(BF16)
        dv = (dv_ref[...] * SCALE).astype(BF16)
        out_ref[:, 0:KROWS, :] = dk.reshape(NSP, KROWS, DH)
        out_ref[:, KROWS : 2 * KROWS, :] = dv.reshape(NSP, KROWS, DH)


OUT_ROWS = 2 * KROWS + QROWS
UNROLL = 2
ORDER = (4, -3, 3, -2, 2, -1, 1, 0)


def grads_call(last, tab, parts, kv, sums, arrived):
    pairs = QB * KLEN
    whole = pl.BlockSpec((KLEN, DH), lambda i, t: (0, 0))
    part = pl.BlockSpec((PART // SHARE, WIDE, DH), lambda i, t: (t[i], 0, 0))
    tile = pl.BlockSpec((1, 8, DH), lambda i, t: (NSP, t[i] // 2, 0))
    dq = pl.BlockSpec((NZ, PART, DH), lambda i, t: (0, 0, 0))
    in_specs = [part] * NZ + [tile] * NZ
    in_specs.append(pl.BlockSpec((NSP, 2 * KROWS, DH), lambda i, t: (0, 0, 0)))
    in_specs += [whole] * len(sums) + [dq] * len(arrived)
    out_specs = [dq]
    out_shape = [jax.ShapeDtypeStruct((NZ, PART, DH), F32 if last else BF16)]
    scratch = []
    if last:
        out_specs.append(pl.BlockSpec((NSP, OUT_ROWS, DH), lambda i, t: (0, 0, 0)))
        out_shape.append(jax.ShapeDtypeStruct((NSP, OUT_ROWS, DH), BF16))
        scratch = [pltpu.VMEM((KLEN, DH), F32)] * 2
    else:
        out_specs += [whole] * 2
        out_shape += [jax.ShapeDtypeStruct((KLEN, DH), F32)] * 2
    return pl.pallas_call(
        functools.partial(grads, not sums, bool(arrived), last),
        grid_spec=pltpu.PrefetchScalarGridSpec(
            num_scalar_prefetch=1,
            grid=(1,),
            in_specs=in_specs,
            out_specs=out_specs,
            scratch_shapes=[*scratch, pltpu.VMEM((QB, DH), F32)],
        ),
        out_shape=out_shape,
        compiler_params=pltpu.CompilerParams(vmem_limit_bytes=26 << 20),
        cost_estimate=cost(pairs * 10 * DH, 4 << 20, pairs),
        name="grads",
    )(tab, *parts, *parts, kv, *sums, *arrived)


def unpack(x_ref, *refs):
    outs, bufs, sems = refs[:3], refs[3:6], refs[6]
    copies = []
    pieces = [(0, 0, QROWS, 2 * KROWS)]
    for n in (1, 2):
        for r in range(0, KROWS, KROWS // 2):
            pieces.append((n, r, KROWS // 2, (n - 1) * KROWS + r))
    for p, (n, r, rows, at) in enumerate(pieces):
        for h in range(H):
            bufs[n][r : r + rows, h * DH : (h + 1) * DH] = x_ref[h, at : at + rows, :].astype(F32)
        copy = pltpu.make_async_copy(
            bufs[n].at[r : r + rows], outs[n].at[r : r + rows], sems.at[p]
        )
        copy.start()
        copies.append(copy)
    for copy in copies:
        copy.wait()


def unpacked(x):
    shapes = [(QROWS, H * DH), (KROWS, H * DH), (KROWS, H * DH)]
    return pl.pallas_call(
        unpack,
        in_specs=[pl.BlockSpec(memory_space=pltpu.VMEM)],
        out_specs=[pl.BlockSpec(memory_space=pl.ANY)] * 3,
        out_shape=[jax.ShapeDtypeStruct(shape, F32) for shape in shapes],
        scratch_shapes=[pltpu.VMEM(shape, F32) for shape in shapes]
        + [pltpu.SemaphoreType.DMA((5,))],
        compiler_params=pltpu.CompilerParams(vmem_limit_bytes=8 << 20),
        cost_estimate=cost(10**6, 3 * 10**6),
        name="unpack",
    )(x)


def turn(x, by):
    pairs = []
    for z in range(NZ):
        for c in range(2):
            pairs.append((z * 2 + c, (z + (1 - 2 * c) * by) % NZ * 2 + c))
    return lax.ppermute(x, ("z", "c"), pairs)


def regroup(x):
    return lax.all_to_all(x, PLANE, split_axis=0, concat_axis=0, tiled=True)


def body(queries, keys, values, outputs, out_grad, stats):
    z = lax.axis_index("z")
    b = lax.axis_index(("y", "xh")).astype(jnp.int32).reshape(1)
    own = packed_queries(b, queries, out_grad, outputs, stats)
    own = regroup(own)
    kv = packed_keys(keys, values)
    kv = regroup(kv)
    own = with_stats(own)

    one, two = [own], [own]
    for n in range(1, NZ // 2 + 1):
        one.append(turn(one[-1], 1))
        if n < NZ // 2:
            two.append(turn(two[-1], -1))
    parts = one[::-1] + two[1:]
    half = NZ // 2
    sign = 1 - 2 * lax.axis_index("c")
    where = (z + sign * jnp.arange(-half, half, dtype=jnp.int32)) % NZ

    chain = {1: (), -1: ()}
    sums = ()
    for to in ORDER:
        tab = jnp.concatenate([((z + sign * to) % NZ).reshape(1), where]).astype(jnp.int32)
        way = 1 if to > 0 else -1
        dq, *sums = grads_call(to == 0, tab, parts, kv, sums, chain[way] if to else ())
        if to:
            chain[way] = (turn(dq, way),)
    mine = dq + (chain[1][0].astype(F32) + chain[-1][0].astype(F32))
    mine = (mine * (ROOT * SCALE)).reshape(NKV, NXC, QROWS, DH)
    mine = jnp.swapaxes(mine, 0, 1).reshape(NSP, QROWS, DH).astype(BF16)
    packed = lax.dynamic_update_slice(sums[0], mine, (0, 2 * KROWS, 0))
    packed = regroup(packed)
    return unpacked(packed)


def solution(mesh):
    torus = Mesh(mesh.devices.reshape(NY, NX, NZ, 2, 2), ALL)
    return jax.shard_map(
        body,
        mesh=torus,
        in_specs=(P(SP), P(ALL), P(ALL), P(SP), P(SP), P(SP)),
        out_specs=(P(ALL), P(ALL), P(ALL)),
        check_vma=False,
    )
```

```python
import math

import jax
import jax.numpy as jnp
from jax import lax
from jax.experimental import pallas as pl
from jax.experimental.pallas import tpu as pltpu
from jax.sharding import Mesh
from jax.sharding import PartitionSpec as P


H = 32
DH = 128
QLEN = 4096
KLEN = 2048
NY, NX, NZ = 4, 2, 8
NKV = NY * NX
SP = ("z", "xl", "c")
ALL = ("y", "xh", "z", "xl", "c")
PLANE = ("xl", "c", "y", "xh")
NSP = 32
NXC = 4
ROWS = QLEN // NSP
SHARE = ROWS // NKV
WIDE = 2 * SHARE
TALL = WIDE + 8
KROWS = KLEN // NSP
QB = QLEN // NZ
PART = QB // NZ
QROWS = QB // NSP
LOG2E = math.log2(math.e)
ROOT = 1.0 / math.sqrt(DH)
SCALE = 1.0 / (KLEN * NKV)
F32 = jnp.float32
BF16 = jnp.bfloat16


def dot(a, b, dims):
    return lax.dot_general(a, b, ((dims[0], dims[1]), ((), ())), preferred_element_type=F32)


def cost(flops, size, trans=0):
    return pl.CostEstimate(flops=flops, bytes_accessed=size, transcendentals=trans)


def three(x):
    hi = x.astype(BF16).astype(F32)
    mid = (x - hi).astype(BF16).astype(F32)
    return hi, mid, x - hi - mid


def pack_queries(b_ref, q_ref, g_ref, o_ref, s_ref, out_ref):
    cols = []
    for h in range(H):
        c = slice(h * DH, (h + 1) * DH)
        out_ref[h, 0:SHARE, :] = q_ref[:, c]
        out_ref[h, SHARE:WIDE, :] = g_ref[:, c]
        prod = g_ref[:, c].astype(F32) * o_ref[:, c].astype(F32)
        cols.append(jnp.sum(prod, axis=1, keepdims=True))
    delta = jnp.transpose(jnp.concatenate(cols, axis=1))
    lane = lax.broadcasted_iota(jnp.int32, (H, DH), 1)
    here = lane // SHARE == b_ref[0]
    row = lax.broadcasted_iota(jnp.int32, (H, 8, DH), 1)
    tile = jnp.zeros((H, 8, DH), F32)
    delta = jnp.concatenate([delta] * NKV, axis=1)
    for r, x in enumerate(three(s_ref[...] * LOG2E) + three(delta)):
        x = jnp.where(here, x, 0.0)
        tile = jnp.where(row == r, x[:, None, :], tile)
    out_ref[:, WIDE:TALL, :] = tile.astype(BF16)


def packed_queries(b, queries, out_grad, outputs, stats):
    wide = pl.BlockSpec((SHARE, H * DH), lambda i, b: (b[0], 0))
    return pl.pallas_call(
        pack_queries,
        grid_spec=pltpu.PrefetchScalarGridSpec(
            num_scalar_prefetch=1,
            grid=(1,),
            in_specs=[wide, wide, wide, pl.BlockSpec((H, ROWS), lambda i, b: (0, 0))],
            out_specs=pl.BlockSpec((H, TALL, DH), lambda i, b: (0, 0, 0)),
        ),
        out_shape=jax.ShapeDtypeStruct((H, TALL, DH), BF16),
        cost_estimate=cost(10**6, 10**6),
        name="pack_queries",
    )(b, queries, out_grad, outputs, jnp.transpose(stats))


def gather_stats(x_ref, out_ref):
    out_ref[0:NSP] = x_ref[:, 0:WIDE, :]
    tile = x_ref[:, WIDE:TALL, :].astype(F32).reshape(NXC, NKV, 8, DH)
    out_ref[NSP] = jnp.sum(tile, axis=1).reshape(WIDE, DH).astype(BF16)


def with_stats(x):
    return pl.pallas_call(
        gather_stats,
        out_shape=jax.ShapeDtypeStruct((NSP + 1, WIDE, DH), BF16),
        compiler_params=pltpu.CompilerParams(vmem_limit_bytes=8 << 20),
        cost_estimate=cost(10**6, 10**6),
        name="gather_stats",
    )(x)


def pack_keys(k_ref, v_ref, out_ref):
    for h in range(H):
        c = slice(h * DH, (h + 1) * DH)
        out_ref[h, 0:KROWS, :] = k_ref[:, c]
        out_ref[h, KROWS : 2 * KROWS, :] = v_ref[:, c]


def packed_keys(keys, values):
    return pl.pallas_call(
        pack_keys,
        out_shape=jax.ShapeDtypeStruct((H, 2 * KROWS, DH), BF16),
        cost_estimate=cost(10**6, 2 * 10**6),
        name="pack_keys",
    )(keys, values)


def queries_of(to_z, parts, tiles):
    q = jnp.concatenate([p[:, 0:SHARE, :].reshape(PART, DH) for p in parts], axis=0)
    g = jnp.concatenate([p[:, SHARE:WIDE, :].reshape(PART, DH) for p in parts], axis=0)
    st, de = [], []
    for tile in tiles:
        x = tile[0].astype(F32)
        x = jnp.where(to_z % 2 == 0, x[:, :PART], x[:, PART:])
        st.append(x[0:1] + x[1:2] + x[2:3])
        de.append(x[3:4] + x[4:5] + x[5:6])
    return q, g, jnp.concatenate(st, axis=1), jnp.concatenate(de, axis=1)


def block_grads(to_z, parts, tiles, kv_ref, dk_ref, dv_ref):
    q, g, st, de = queries_of(to_z, parts, tiles)
    per = 8
    bk = per * KROWS
    total = None
    for j in range(NSP // per):
        k = kv_ref[j * per : (j + 1) * per, 0:KROWS, :].reshape(bk, DH)
        v = kv_ref[j * per : (j + 1) * per, KROWS : 2 * KROWS, :].reshape(bk, DH)
        at = slice(j * bk, (j + 1) * bk)
        p = jnp.exp2(dot(k, q, ((1,), (1,))) * (ROOT * LOG2E) - st)
        ds = (p * (dot(v, g, ((1,), (1,))) - de)).astype(BF16)
        dv_ref[at, :] += dot(p.astype(BF16), g, ((1,), (0,)))
        dk_ref[at, :] += dot(ds, q, ((1,), (0,)))
        part = dot(ds, k, ((0,), (0,)))
        total = part if total is None else total + part
    return total.reshape(NZ, PART, DH)


def grads(tab, *refs):
    parts = refs[:NZ]
    tiles = refs[NZ : 2 * NZ]
    kv_ref = refs[2 * NZ]
    dq_refs = refs[2 * NZ + 1 : 3 * NZ + 1]
    out_ref, dk_ref, dv_ref = refs[3 * NZ + 1 :]
    step = pl.program_id(0)

    @pl.when(step == 0)
    def _():
        dk_ref[...] = jnp.zeros_like(dk_ref)
        dv_ref[...] = jnp.zeros_like(dv_ref)

    total = block_grads(tab[step], parts, tiles, kv_ref, dk_ref, dv_ref)
    for n, dq_ref in enumerate(dq_refs):

        @pl.when(step == n)
        def _(dq_ref=dq_ref):
            for j in range(NZ):
                dq_ref[tab[NZ + j]] = total[j].astype(dq_ref.dtype)

    @pl.when(step == NZ - 1)
    def _():
        dk = (dk_ref[...] * (ROOT * SCALE)).astype(BF16)
        dv = (dv_ref[...] * SCALE).astype(BF16)
        out_ref[:, 0:KROWS, :] = dk.reshape(NSP, KROWS, DH)
        out_ref[:, KROWS : 2 * KROWS, :] = dv.reshape(NSP, KROWS, DH)


ORDER = (4, 3, -3, 2, -2, 1, -1, 0)


def grads_call(tab, parts, kv):
    pairs = QLEN * KLEN
    part = pl.BlockSpec((PART // SHARE, WIDE, DH), lambda i, t: (t[i], 0, 0))
    tile = pl.BlockSpec((1, 8, DH), lambda i, t: (NSP, t[i] // 2, 0))
    keys = pl.BlockSpec((NSP, 2 * KROWS, DH), lambda i, t: (0, 0, 0))
    dq = pl.BlockSpec((NZ, PART, DH), lambda i, t: (0, 0, 0))
    return pl.pallas_call(
        grads,
        grid_spec=pltpu.PrefetchScalarGridSpec(
            num_scalar_prefetch=1,
            grid=(NZ,),
            in_specs=[part] * NZ + [tile] * NZ + [keys],
            out_specs=[dq] * NZ + [keys],
            scratch_shapes=[pltpu.VMEM((KLEN, DH), F32)] * 2,
        ),
        out_shape=[
            pltpu.HBM((NZ, PART, DH), BF16) if to else jax.ShapeDtypeStruct((NZ, PART, DH), F32)
            for to in ORDER
        ]
        + [jax.ShapeDtypeStruct((NSP, 2 * KROWS, DH), BF16)],
        compiler_params=pltpu.CompilerParams(vmem_limit_bytes=26 << 20),
        cost_estimate=cost(pairs * 10 * DH, 8 << 20, pairs),
        name="grads",
    )(tab, *parts, *parts, kv)


def unpack_keys(x_ref, *refs):
    outs, bufs, sems = refs[:2], refs[2:4], refs[4]
    copies = []
    some = KROWS // 2
    for n in range(2):
        for r in range(0, KROWS, some):
            at = n * KROWS + r
            for h in range(H):
                bufs[n][r : r + some, h * DH : (h + 1) * DH] = x_ref[
                    h, at : at + some, :
                ].astype(F32)
            copy = pltpu.make_async_copy(
                bufs[n].at[r : r + some], outs[n].at[r : r + some], sems.at[len(copies)]
            )
            copy.start()
            copies.append(copy)
    for copy in copies:
        copy.wait()


def unpacked_keys(x):
    shape = (KROWS, H * DH)
    return pl.pallas_call(
        unpack_keys,
        in_specs=[pl.BlockSpec(memory_space=pltpu.VMEM)],
        out_specs=[pl.BlockSpec(memory_space=pl.ANY)] * 2,
        out_shape=[jax.ShapeDtypeStruct(shape, F32)] * 2,
        scratch_shapes=[pltpu.VMEM(shape, F32)] * 2 + [pltpu.SemaphoreType.DMA((4,))],
        compiler_params=pltpu.CompilerParams(vmem_limit_bytes=8 << 20),
        cost_estimate=cost(10**6, 3 * 10**6),
        name="unpack_keys",
    )(x)


def unpack_queries(x_ref, dq_ref):
    for h in range(H):
        dq_ref[:, h * DH : (h + 1) * DH] = x_ref[h].astype(F32)


def unpacked_queries(x):
    return pl.pallas_call(
        unpack_queries,
        out_shape=jax.ShapeDtypeStruct((QROWS, H * DH), F32),
        compiler_params=pltpu.CompilerParams(vmem_limit_bytes=4 << 20),
        cost_estimate=cost(10**6, 10**6),
        name="unpack_queries",
    )(x)


def turn(x, by):
    pairs = []
    for z in range(NZ):
        for c in range(2):
            pairs.append((z * 2 + c, (z + (1 - 2 * c) * by) % NZ * 2 + c))
    return lax.ppermute(x, ("z", "c"), pairs)


def regroup(x):
    return lax.all_to_all(x, PLANE, split_axis=0, concat_axis=0, tiled=True)


def body(queries, keys, values, outputs, out_grad, stats):
    z = lax.axis_index("z")
    b = lax.axis_index(("y", "xh")).astype(jnp.int32).reshape(1)
    own = packed_queries(b, queries, out_grad, outputs, stats)
    own = regroup(own)
    kv = packed_keys(keys, values)
    kv = regroup(kv)
    own = with_stats(own)

    one, two = [own], [own]
    for n in range(1, NZ // 2 + 1):
        one.append(turn(one[-1], 1))
        if n < NZ // 2:
            two.append(turn(two[-1], -1))
    parts = one[::-1] + two[1:]
    half = NZ // 2
    sign = 1 - 2 * lax.axis_index("c")
    where = (z + sign * jnp.arange(-half, half, dtype=jnp.int32)) % NZ

    tab = jnp.concatenate([(z + sign * jnp.array(ORDER, jnp.int32)) % NZ, where])
    *dqs, mine, packed = grads_call(tab.astype(jnp.int32), parts, kv)
    packed = regroup(packed)
    for n, dq in enumerate(dqs):
        mine = mine + turn(dq, ORDER[n]).astype(F32)
    mine = (mine * (ROOT * SCALE)).reshape(NKV, NXC, QROWS, DH)
    mine = jnp.swapaxes(mine, 0, 1).reshape(NSP, QROWS, DH).astype(BF16)
    mine = regroup(mine)
    dk, dv = unpacked_keys(packed)
    return unpacked_queries(mine), dk, dv


def solution(mesh):
    torus = Mesh(mesh.devices.reshape(NY, NX, NZ, 2, 2), ALL)
    return jax.shard_map(
        body,
        mesh=torus,
        in_specs=(P(SP), P(ALL), P(ALL), P(SP), P(SP), P(SP)),
        out_specs=(P(ALL), P(ALL), P(ALL)),
        check_vma=False,
    )
```

```python
import functools
import math

import jax
import jax.numpy as jnp
from jax import lax
from jax.experimental import pallas as pl
from jax.experimental.pallas import tpu as pltpu
from jax.sharding import Mesh
from jax.sharding import PartitionSpec as P


H = 32
DH = 128
QLEN = 4096
KLEN = 2048
NY, NX, NZ = 4, 2, 8
NKV = NY * NX
SP = ("z", "xl", "c")
ALL = ("y", "xh", "z", "xl", "c")
PLANE = ("xl", "c", "y", "xh")
NSP = 32
NXC = 4
ROWS = QLEN // NSP
SHARE = ROWS // NKV
WIDE = 2 * SHARE
TALL = WIDE + 8
KROWS = KLEN // NSP
QB = QLEN // NZ
PART = QB // NZ
QROWS = QB // NSP
LOG2E = math.log2(math.e)
ROOT = 1.0 / math.sqrt(DH)
SCALE = 1.0 / (KLEN * NKV)
F32 = jnp.float32
BF16 = jnp.bfloat16


def dot(a, b, dims):
    return lax.dot_general(a, b, ((dims[0], dims[1]), ((), ())), preferred_element_type=F32)


def cost(flops, size, trans=0):
    return pl.CostEstimate(flops=flops, bytes_accessed=size, transcendentals=trans)


def three(x):
    hi = x.astype(BF16).astype(F32)
    mid = (x - hi).astype(BF16).astype(F32)
    return hi, mid, x - hi - mid


def pack_queries(b_ref, q_ref, g_ref, o_ref, s_ref, out_ref):
    cols = []
    for h in range(H):
        c = slice(h * DH, (h + 1) * DH)
        out_ref[h, 0:SHARE, :] = q_ref[:, c]
        out_ref[h, SHARE:WIDE, :] = g_ref[:, c]
        prod = g_ref[:, c].astype(F32) * o_ref[:, c].astype(F32)
        cols.append(jnp.sum(prod, axis=1, keepdims=True))
    delta = jnp.transpose(jnp.concatenate(cols, axis=1))
    lane = lax.broadcasted_iota(jnp.int32, (H, DH), 1)
    here = lane // SHARE == b_ref[0]
    row = lax.broadcasted_iota(jnp.int32, (H, 8, DH), 1)
    tile = jnp.zeros((H, 8, DH), F32)
    delta = jnp.concatenate([delta] * NKV, axis=1)
    for r, x in enumerate(three(s_ref[...] * LOG2E) + three(delta)):
        x = jnp.where(here, x, 0.0)
        tile = jnp.where(row == r, x[:, None, :], tile)
    out_ref[:, WIDE:TALL, :] = tile.astype(BF16)


def packed_queries(b, queries, out_grad, outputs, stats):
    wide = pl.BlockSpec((SHARE, H * DH), lambda i, b: (b[0], 0))
    return pl.pallas_call(
        pack_queries,
        grid_spec=pltpu.PrefetchScalarGridSpec(
            num_scalar_prefetch=1,
            grid=(1,),
            in_specs=[wide, wide, wide, pl.BlockSpec((H, ROWS), lambda i, b: (0, 0))],
            out_specs=pl.BlockSpec((H, TALL, DH), lambda i, b: (0, 0, 0)),
        ),
        out_shape=jax.ShapeDtypeStruct((H, TALL, DH), BF16),
        cost_estimate=cost(10**6, 10**6),
        name="pack_queries",
    )(b, queries, out_grad, outputs, jnp.transpose(stats))


def gather_stats(x_ref, out_ref):
    out_ref[0:NSP] = x_ref[:, 0:WIDE, :]
    tile = x_ref[:, WIDE:TALL, :].astype(F32).reshape(NXC, NKV, 8, DH)
    out_ref[NSP] = jnp.sum(tile, axis=1).reshape(WIDE, DH).astype(BF16)


def with_stats(x):
    return pl.pallas_call(
        gather_stats,
        out_shape=jax.ShapeDtypeStruct((NSP + 1, WIDE, DH), BF16),
        compiler_params=pltpu.CompilerParams(vmem_limit_bytes=8 << 20),
        cost_estimate=cost(10**6, 10**6),
        name="gather_stats",
    )(x)


def pack_keys(k_ref, v_ref, out_ref):
    for h in range(H):
        c = slice(h * DH, (h + 1) * DH)
        out_ref[h, 0:KROWS, :] = k_ref[:, c]
        out_ref[h, KROWS : 2 * KROWS, :] = v_ref[:, c]


def packed_keys(keys, values):
    return pl.pallas_call(
        pack_keys,
        out_shape=jax.ShapeDtypeStruct((H, 2 * KROWS, DH), BF16),
        cost_estimate=cost(10**6, 2 * 10**6),
        name="pack_keys",
    )(keys, values)


def queries_of(to_z, parts, tiles):
    q = jnp.concatenate([p[:, 0:SHARE, :].reshape(PART, DH) for p in parts], axis=0)
    g = jnp.concatenate([p[:, SHARE:WIDE, :].reshape(PART, DH) for p in parts], axis=0)
    st, de = [], []
    for tile in tiles:
        x = tile[0].astype(F32)
        x = jnp.where(to_z % 2 == 0, x[:, :PART], x[:, PART:])
        st.append(x[0:1] + x[1:2] + x[2:3])
        de.append(x[3:4] + x[4:5] + x[5:6])
    return q, g, jnp.concatenate(st, axis=1), jnp.concatenate(de, axis=1)


def block_grads(to_z, parts, tiles, kv_ref, dk_ref, dv_ref):
    q, g, st, de = queries_of(to_z, parts, tiles)
    per = 8
    bk = per * KROWS
    total = None
    for j in range(NSP // per):
        k = kv_ref[j * per : (j + 1) * per, 0:KROWS, :].reshape(bk, DH)
        v = kv_ref[j * per : (j + 1) * per, KROWS : 2 * KROWS, :].reshape(bk, DH)
        at = slice(j * bk, (j + 1) * bk)
        p = jnp.exp2(dot(k, q, ((1,), (1,))) * (ROOT * LOG2E) - st)
        ds = (p * (dot(v, g, ((1,), (1,))) - de)).astype(BF16)
        dv_ref[at, :] += dot(p.astype(BF16), g, ((1,), (0,)))
        dk_ref[at, :] += dot(ds, q, ((1,), (0,)))
        part = dot(ds, k, ((0,), (0,)))
        total = part if total is None else total + part
    return total.reshape(NZ, PART, DH)


def grads(count, first, last, added, tab, *refs):
    parts = refs[:NZ]
    tiles = refs[NZ : 2 * NZ]
    kv_ref = refs[2 * NZ]
    rest = refs[2 * NZ + 1 :]
    if not first:
        dk_in, dv_in = rest[:2]
        rest = rest[2:]
    arrived = rest[:count] if added else ()
    rest = rest[len(arrived) :]
    dq_refs = rest[:count]
    dk_ref, dv_ref = rest[-2:]
    step = pl.program_id(0)

    @pl.when(step == 0)
    def _():
        dk_ref[...] = jnp.zeros_like(dk_ref) if first else dk_in[...]
        dv_ref[...] = jnp.zeros_like(dv_ref) if first else dv_in[...]

    total = block_grads(tab[step], parts, tiles, kv_ref, dk_ref, dv_ref)
    for n, dq_ref in enumerate(dq_refs):

        @pl.when(step == n)
        def _(n=n, dq_ref=dq_ref):
            for j in range(NZ):
                at = tab[count + j]
                part = total[j]
                if added:
                    part = part + arrived[n][at].astype(F32)
                dq_ref[at] = part.astype(dq_ref.dtype)

    if last:
        out_ref = rest[count]

        @pl.when(step == count - 1)
        def _():
            dk = (dk_ref[...] * (ROOT * SCALE)).astype(BF16)
            dv = (dv_ref[...] * SCALE).astype(BF16)
            out_ref[:, 0:KROWS, :] = dk.reshape(NSP, KROWS, DH)
            out_ref[:, KROWS : 2 * KROWS, :] = dv.reshape(NSP, KROWS, DH)


OUT_ROWS = 2 * KROWS + QROWS


def grads_call(count, first, last, tab, parts, kv, sums=(), arrived=()):
    pairs = count * QB * KLEN
    whole = pl.BlockSpec((KLEN, DH), lambda i, t: (0, 0))
    part = pl.BlockSpec((PART // SHARE, WIDE, DH), lambda i, t: (t[i], 0, 0))
    tile = pl.BlockSpec((1, 8, DH), lambda i, t: (NSP, t[i] // 2, 0))
    in_specs = [part] * NZ + [tile] * NZ
    in_specs.append(pl.BlockSpec((NSP, 2 * KROWS, DH), lambda i, t: (0, 0, 0)))
    dq = pl.BlockSpec((NZ, PART, DH), lambda i, t: (0, 0, 0))
    out_specs = [dq] * count
    out_shape = [jax.ShapeDtypeStruct((NZ, PART, DH), F32 if last else BF16)] * count
    scratch = []
    if last:
        out_specs.append(pl.BlockSpec((NSP, OUT_ROWS, DH), lambda i, t: (0, 0, 0)))
        out_shape.append(jax.ShapeDtypeStruct((NSP, OUT_ROWS, DH), BF16))
        scratch = [pltpu.VMEM((KLEN, DH), F32)] * 2
    else:
        out_specs += [whole] * 2
        out_shape += [jax.ShapeDtypeStruct((KLEN, DH), F32)] * 2
    return pl.pallas_call(
        functools.partial(grads, count, first, last, bool(arrived)),
        grid_spec=pltpu.PrefetchScalarGridSpec(
            num_scalar_prefetch=1,
            grid=(count,),
            in_specs=in_specs + [whole] * len(sums) + [dq] * len(arrived),
            out_specs=out_specs,
            scratch_shapes=scratch,
        ),
        out_shape=out_shape,
        compiler_params=pltpu.CompilerParams(vmem_limit_bytes=26 << 20),
        cost_estimate=cost(pairs * 10 * DH, 4 << 20, pairs),
        name="grads",
    )(tab, *parts, *parts, kv, *sums, *arrived)


def unpack(x_ref, *refs):
    outs, bufs, sems = refs[:3], refs[3:6], refs[6]
    copies = []
    pieces = [(0, 0, QROWS, 2 * KROWS)]
    for n in (1, 2):
        for r in range(0, KROWS, KROWS // 2):
            pieces.append((n, r, KROWS // 2, (n - 1) * KROWS + r))
    for p, (n, r, rows, at) in enumerate(pieces):
        for h in range(H):
            bufs[n][r : r + rows, h * DH : (h + 1) * DH] = x_ref[h, at : at + rows, :].astype(F32)
        copy = pltpu.make_async_copy(
            bufs[n].at[r : r + rows], outs[n].at[r : r + rows], sems.at[p]
        )
        copy.start()
        copies.append(copy)
    for copy in copies:
        copy.wait()


def unpacked(x):
    shapes = [(QROWS, H * DH), (KROWS, H * DH), (KROWS, H * DH)]
    return pl.pallas_call(
        unpack,
        in_specs=[pl.BlockSpec(memory_space=pltpu.VMEM)],
        out_specs=[pl.BlockSpec(memory_space=pl.ANY)] * 3,
        out_shape=[jax.ShapeDtypeStruct(shape, F32) for shape in shapes],
        scratch_shapes=[pltpu.VMEM(shape, F32) for shape in shapes]
        + [pltpu.SemaphoreType.DMA((5,))],
        compiler_params=pltpu.CompilerParams(vmem_limit_bytes=8 << 20),
        cost_estimate=cost(10**6, 3 * 10**6),
        name="unpack",
    )(x)


def turn(x, by):
    pairs = []
    for z in range(NZ):
        for c in range(2):
            pairs.append((z * 2 + c, (z + (1 - 2 * c) * by) % NZ * 2 + c))
    return lax.ppermute(x, ("z", "c"), pairs)


def regroup(x):
    return lax.all_to_all(x, PLANE, split_axis=0, concat_axis=0, tiled=True)


def body(queries, keys, values, outputs, out_grad, stats):
    z = lax.axis_index("z")
    b = lax.axis_index(("y", "xh")).astype(jnp.int32).reshape(1)
    own = packed_queries(b, queries, out_grad, outputs, stats)
    own = regroup(own)
    kv = packed_keys(keys, values)
    kv = regroup(kv)
    own = with_stats(own)

    one, two = [own], [own]
    for n in range(1, NZ // 2 + 1):
        one.append(turn(one[-1], 1))
        if n < NZ // 2:
            two.append(turn(two[-1], -1))
    parts = one[::-1] + two[1:]
    half = NZ // 2
    sign = 1 - 2 * lax.axis_index("c")
    where = (z + sign * jnp.arange(-half, half, dtype=jnp.int32)) % NZ

    def call(group, sums, arrived=()):
        tab = jnp.concatenate([(z + sign * jnp.array(group, jnp.int32)) % NZ, where])
        out = grads_call(
            len(group), not sums, 0 in group, tab.astype(jnp.int32), parts, kv, sums, arrived
        )
        return out[: len(group)], out[len(group) :]

    (four, back3), sums = call((4, -3), ())
    arrived = (turn(four, 1), turn(back3, -1))
    (two, one, back1), sums = call((2, 1, -1), sums)
    sent = [turn(two, 2), turn(one, 1), turn(back1, -1)]
    (three, back2), sums = call((3, -2), sums, arrived)
    sent += [turn(three, 3), turn(back2, -2)]
    (mine,), sums = call((0,), sums)
    mine = mine + sum(x.astype(F32) for x in sent)
    mine = (mine * (ROOT * SCALE)).reshape(NKV, NXC, QROWS, DH)
    mine = jnp.swapaxes(mine, 0, 1).reshape(NSP, QROWS, DH).astype(BF16)
    packed = lax.dynamic_update_slice(sums[0], mine, (0, 2 * KROWS, 0))
    packed = regroup(packed)
    return unpacked(packed)


def solution(mesh):
    torus = Mesh(mesh.devices.reshape(NY, NX, NZ, 2, 2), ALL)
    return jax.shard_map(
        body,
        mesh=torus,
        in_specs=(P(SP), P(ALL), P(ALL), P(SP), P(SP), P(SP)),
        out_specs=(P(ALL), P(ALL), P(ALL)),
        check_vma=False,
    )
```

```python
import functools
import math

import jax
import jax.numpy as jnp
from jax import lax
from jax.experimental import pallas as pl
from jax.experimental.pallas import tpu as pltpu
from jax.sharding import Mesh
from jax.sharding import PartitionSpec as P


H = 32
DH = 128
QLEN = 4096
KLEN = 2048
NY, NX, NZ = 4, 2, 8
NKV = NY * NX
SP = ("z", "xl", "c")
ALL = ("y", "xh", "z", "xl", "c")
PLANE = ("xl", "c", "y", "xh")
NSP = 32
NXC = 4
ROWS = QLEN // NSP
SHARE = ROWS // NKV
WIDE = 2 * SHARE
TALL = WIDE + 8
KROWS = KLEN // NSP
QB = QLEN // NZ
PART = QB // NZ
QROWS = QB // NSP
LOG2E = math.log2(math.e)
ROOT = 1.0 / math.sqrt(DH)
SCALE = 1.0 / (KLEN * NKV)
F32 = jnp.float32
BF16 = jnp.bfloat16


def dot(a, b, dims):
    return lax.dot_general(a, b, ((dims[0], dims[1]), ((), ())), preferred_element_type=F32)


def cost(flops, size, trans=0):
    return pl.CostEstimate(flops=flops, bytes_accessed=size, transcendentals=trans)


def three(x):
    hi = x.astype(BF16).astype(F32)
    mid = (x - hi).astype(BF16).astype(F32)
    return hi, mid, x - hi - mid


def pack_queries(b_ref, q_ref, g_ref, o_ref, s_ref, out_ref):
    cols = []
    for h in range(H):
        c = slice(h * DH, (h + 1) * DH)
        out_ref[h, 0:SHARE, :] = q_ref[:, c]
        out_ref[h, SHARE:WIDE, :] = g_ref[:, c]
        prod = g_ref[:, c].astype(F32) * o_ref[:, c].astype(F32)
        cols.append(jnp.sum(prod, axis=1, keepdims=True))
    delta = jnp.transpose(jnp.concatenate(cols, axis=1))
    lane = lax.broadcasted_iota(jnp.int32, (H, DH), 1)
    here = lane // SHARE == b_ref[0]
    row = lax.broadcasted_iota(jnp.int32, (H, 8, DH), 1)
    tile = jnp.zeros((H, 8, DH), F32)
    delta = jnp.concatenate([delta] * NKV, axis=1)
    for r, x in enumerate(three(s_ref[...] * LOG2E) + three(delta)):
        x = jnp.where(here, x, 0.0)
        tile = jnp.where(row == r, x[:, None, :], tile)
    out_ref[:, WIDE:TALL, :] = tile.astype(BF16)


def packed_queries(b, queries, out_grad, outputs, stats):
    wide = pl.BlockSpec((SHARE, H * DH), lambda i, b: (b[0], 0))
    return pl.pallas_call(
        pack_queries,
        grid_spec=pltpu.PrefetchScalarGridSpec(
            num_scalar_prefetch=1,
            grid=(1,),
            in_specs=[wide, wide, wide, pl.BlockSpec((H, ROWS), lambda i, b: (0, 0))],
            out_specs=pl.BlockSpec((H, TALL, DH), lambda i, b: (0, 0, 0)),
        ),
        out_shape=jax.ShapeDtypeStruct((H, TALL, DH), BF16),
        cost_estimate=cost(10**6, 10**6),
        name="pack_queries",
    )(b, queries, out_grad, outputs, jnp.transpose(stats))


def gather_stats(x_ref, out_ref):
    out_ref[0:NSP] = x_ref[:, 0:WIDE, :]
    tile = x_ref[:, WIDE:TALL, :].astype(F32).reshape(NXC, NKV, 8, DH)
    out_ref[NSP] = jnp.sum(tile, axis=1).reshape(WIDE, DH).astype(BF16)


def with_stats(x):
    return pl.pallas_call(
        gather_stats,
        out_shape=jax.ShapeDtypeStruct((NSP + 1, WIDE, DH), BF16),
        compiler_params=pltpu.CompilerParams(vmem_limit_bytes=8 << 20),
        cost_estimate=cost(10**6, 10**6),
        name="gather_stats",
    )(x)


def pack_keys(k_ref, v_ref, out_ref):
    for h in range(H):
        c = slice(h * DH, (h + 1) * DH)
        out_ref[h, 0:KROWS, :] = k_ref[:, c]
        out_ref[h, KROWS : 2 * KROWS, :] = v_ref[:, c]


def packed_keys(keys, values):
    return pl.pallas_call(
        pack_keys,
        out_shape=jax.ShapeDtypeStruct((H, 2 * KROWS, DH), BF16),
        cost_estimate=cost(10**6, 2 * 10**6),
        name="pack_keys",
    )(keys, values)


def queries_of(to_z, parts, tiles):
    q = jnp.concatenate([p[:, 0:SHARE, :].reshape(PART, DH) for p in parts], axis=0)
    g = jnp.concatenate([p[:, SHARE:WIDE, :].reshape(PART, DH) for p in parts], axis=0)
    st, de = [], []
    for tile in tiles:
        x = tile[0].astype(F32)
        x = jnp.where(to_z % 2 == 0, x[:, :PART], x[:, PART:])
        st.append(x[0:1] + x[1:2] + x[2:3])
        de.append(x[3:4] + x[4:5] + x[5:6])
    return q, g, jnp.concatenate(st, axis=1), jnp.concatenate(de, axis=1)


def block_grads(to_z, parts, tiles, kv_ref, dk_ref, dv_ref):
    q, g, st, de = queries_of(to_z, parts, tiles)
    per = 8
    bk = per * KROWS
    total = None
    for j in range(NSP // per):
        k = kv_ref[j * per : (j + 1) * per, 0:KROWS, :].reshape(bk, DH)
        v = kv_ref[j * per : (j + 1) * per, KROWS : 2 * KROWS, :].reshape(bk, DH)
        at = slice(j * bk, (j + 1) * bk)
        p = jnp.exp2(dot(k, q, ((1,), (1,))) * (ROOT * LOG2E) - st)
        ds = (p * (dot(v, g, ((1,), (1,))) - de)).astype(BF16)
        dv_ref[at, :] += dot(p.astype(BF16), g, ((1,), (0,)))
        dk_ref[at, :] += dot(ds, q, ((1,), (0,)))
        part = dot(ds, k, ((0,), (0,)))
        total = part if total is None else total + part
    return total.reshape(NZ, PART, DH)


def grads(count, first, last, added, tab, *refs):
    parts = refs[:NZ]
    tiles = refs[NZ : 2 * NZ]
    kv_ref = refs[2 * NZ]
    rest = refs[2 * NZ + 1 :]
    if not first:
        dk_in, dv_in = rest[:2]
        rest = rest[2:]
    arrived = rest[:count] if added else ()
    rest = rest[len(arrived) :]
    dq_refs = rest[:count]
    dk_ref, dv_ref = rest[-2:]
    step = pl.program_id(0)

    @pl.when(step == 0)
    def _():
        dk_ref[...] = jnp.zeros_like(dk_ref) if first else dk_in[...]
        dv_ref[...] = jnp.zeros_like(dv_ref) if first else dv_in[...]

    total = block_grads(tab[step], parts, tiles, kv_ref, dk_ref, dv_ref)
    for n, dq_ref in enumerate(dq_refs):

        @pl.when(step == n)
        def _(n=n, dq_ref=dq_ref):
            for j in range(NZ):
                at = tab[count + j]
                part = total[j].reshape(NXC, QROWS, DH)
                if added:
                    part = part + arrived[n][:, at].astype(F32)
                dq_ref[:, at] = part.astype(dq_ref.dtype)

    if last:
        out_ref = rest[count]

        @pl.when(step == count - 1)
        def _():
            dk = (dk_ref[...] * (ROOT * SCALE)).astype(BF16)
            dv = (dv_ref[...] * SCALE).astype(BF16)
            out_ref[:, 0:KROWS, :] = dk.reshape(NSP, KROWS, DH)
            out_ref[:, KROWS : 2 * KROWS, :] = dv.reshape(NSP, KROWS, DH)


OUT_ROWS = 2 * KROWS + QROWS


def grads_call(count, first, last, tab, parts, kv, sums=(), arrived=()):
    pairs = count * QB * KLEN
    whole = pl.BlockSpec((KLEN, DH), lambda i, t: (0, 0))
    part = pl.BlockSpec((PART // SHARE, WIDE, DH), lambda i, t: (t[i], 0, 0))
    tile = pl.BlockSpec((1, 8, DH), lambda i, t: (NSP, t[i] // 2, 0))
    in_specs = [part] * NZ + [tile] * NZ
    in_specs.append(pl.BlockSpec((NSP, 2 * KROWS, DH), lambda i, t: (0, 0, 0)))
    dq = pl.BlockSpec((NXC, NZ, QROWS, DH), lambda i, t: (0, 0, 0, 0))
    out_specs = [dq] * count
    out_shape = [jax.ShapeDtypeStruct((NXC, NZ, QROWS, DH), F32 if last else BF16)] * count
    scratch = []
    if last:
        out_specs.append(pl.BlockSpec((NSP, OUT_ROWS, DH), lambda i, t: (0, 0, 0)))
        out_shape.append(jax.ShapeDtypeStruct((NSP, OUT_ROWS, DH), BF16))
        scratch = [pltpu.VMEM((KLEN, DH), F32)] * 2
    else:
        out_specs += [whole] * 2
        out_shape += [jax.ShapeDtypeStruct((KLEN, DH), F32)] * 2
    return pl.pallas_call(
        functools.partial(grads, count, first, last, bool(arrived)),
        grid_spec=pltpu.PrefetchScalarGridSpec(
            num_scalar_prefetch=1,
            grid=(count,),
            in_specs=in_specs + [whole] * len(sums) + [dq] * len(arrived),
            out_specs=out_specs,
            scratch_shapes=scratch,
        ),
        out_shape=out_shape,
        compiler_params=pltpu.CompilerParams(vmem_limit_bytes=26 << 20),
        cost_estimate=cost(pairs * 10 * DH, 4 << 20, pairs),
        name="grads",
    )(tab, *parts, *parts, kv, *sums, *arrived)


def unpack(x_ref, *refs):
    outs, bufs, sems = refs[:3], refs[3:6], refs[6]
    copies = []
    pieces = [(0, 0, QROWS, 2 * KROWS)]
    for n in (1, 2):
        for r in range(0, KROWS, KROWS // 2):
            pieces.append((n, r, KROWS // 2, (n - 1) * KROWS + r))
    for p, (n, r, rows, at) in enumerate(pieces):
        for h in range(H):
            bufs[n][r : r + rows, h * DH : (h + 1) * DH] = x_ref[h, at : at + rows, :].astype(F32)
        copy = pltpu.make_async_copy(
            bufs[n].at[r : r + rows], outs[n].at[r : r + rows], sems.at[p]
        )
        copy.start()
        copies.append(copy)
    for copy in copies:
        copy.wait()


def unpacked(x):
    shapes = [(QROWS, H * DH), (KROWS, H * DH), (KROWS, H * DH)]
    return pl.pallas_call(
        unpack,
        in_specs=[pl.BlockSpec(memory_space=pltpu.VMEM)],
        out_specs=[pl.BlockSpec(memory_space=pl.ANY)] * 3,
        out_shape=[jax.ShapeDtypeStruct(shape, F32) for shape in shapes],
        scratch_shapes=[pltpu.VMEM(shape, F32) for shape in shapes]
        + [pltpu.SemaphoreType.DMA((5,))],
        compiler_params=pltpu.CompilerParams(vmem_limit_bytes=8 << 20),
        cost_estimate=cost(10**6, 3 * 10**6),
        name="unpack",
    )(x)


def turn(x, by):
    pairs = []
    for z in range(NZ):
        for c in range(2):
            pairs.append((z * 2 + c, (z + (1 - 2 * c) * by) % NZ * 2 + c))
    return lax.ppermute(x, ("z", "c"), pairs)


def regroup(x):
    return lax.all_to_all(x, PLANE, split_axis=0, concat_axis=0, tiled=True)


def body(queries, keys, values, outputs, out_grad, stats):
    z = lax.axis_index("z")
    b = lax.axis_index(("y", "xh")).astype(jnp.int32).reshape(1)
    own = packed_queries(b, queries, out_grad, outputs, stats)
    own = regroup(own)
    kv = packed_keys(keys, values)
    kv = regroup(kv)
    own = with_stats(own)

    one, two = [own], [own]
    for n in range(1, NZ // 2 + 1):
        one.append(turn(one[-1], 1))
        if n < NZ // 2:
            two.append(turn(two[-1], -1))
    parts = one[::-1] + two[1:]
    half = NZ // 2
    sign = 1 - 2 * lax.axis_index("c")
    where = (z + sign * jnp.arange(-half, half, dtype=jnp.int32)) % NZ

    def call(group, sums, arrived=()):
        tab = jnp.concatenate([(z + sign * jnp.array(group, jnp.int32)) % NZ, where])
        out = grads_call(
            len(group), not sums, 0 in group, tab.astype(jnp.int32), parts, kv, sums, arrived
        )
        return out[: len(group)], out[len(group) :]

    (four, back3), sums = call((4, -3), ())
    arrived = (turn(four, 1), turn(back3, -1))
    (two, one, back1), sums = call((2, 1, -1), sums)
    sent = [turn(two, 2), turn(one, 1), turn(back1, -1)]
    (three, back2), sums = call((3, -2), sums, arrived)
    sent += [turn(three, 3), turn(back2, -2)]
    (mine,), sums = call((0,), sums)
    mine = mine + sum(x.astype(F32) for x in sent)
    mine = (mine * (ROOT * SCALE)).astype(BF16).reshape(NSP, QROWS, DH)
    packed = lax.dynamic_update_slice(sums[0], mine, (0, 2 * KROWS, 0))
    packed = regroup(packed)
    return unpacked(packed)


def solution(mesh):
    torus = Mesh(mesh.devices.reshape(NY, NX, NZ, 2, 2), ALL)
    return jax.shard_map(
        body,
        mesh=torus,
        in_specs=(P(SP), P(ALL), P(ALL), P(SP), P(SP), P(SP)),
        out_specs=(P(ALL), P(ALL), P(ALL)),
        check_vma=False,
    )
```
